256 devices in a mesh: member: 2 (over y_lo), lat: 4 (over x), lon: 32 (over z, y_hi, core).
Axes of the slice: x: 4, y: 4 (y_hi: 2, y_lo: 2; y = y_hi * 2 + y_lo), z: 8, core: 2. Of those that a mesh axis runs over, the one named last changes fastest.
Arguments:
- features: bfloat16 [2, 720, 1440, 128], P('member', 'lat', 'lon'), may hold values from -6 to 6
- present_condition: bfloat16 [2, 720, 1440, 80], P('member', 'lat', 'lon'), may hold values from -6 to 6
- target: bfloat16 [720, 1440, 80], P('lat', 'lon'), may hold values from -8 to 8
- filter_weights_tensor: bfloat16 [3, 3, 128, 80], replicated, may hold values from -0.1875 to 0.1875
Outputs:
- predicted_outputs: bfloat16 [2, 720, 1440, 80], P('member', 'lat', 'lon')
- objective_mean: float32 [], replicated
- hidden_state_slope: bfloat16 [2, 720, 1440, 128], P('member', 'lat', 'lon')
- filter_weights_slope: float32 [3, 3, 128, 80], replicated
The draws below stay inside these ranges and needn't reach their ends.
All inputs are finite; a program needn't handle non-finite values.
Results may differ from the reference program's by a relative error of at most 0.0095.
Values may be sent and summed in bfloat16 or wider, within the bound.
No kernel may reach another device: no remote copies, remote signals or barrier semaphores. Data moves between devices by JAX's collectives and lax.ppermute only.
A program may use at most 128 MiB of HBM per device.

```python
import math
import jax
import jax.numpy as jnp
from jax import lax

C = 128
K = 80
MEMBERS = 2
NLAT = 720
NLON = 1440


def level_of(key, shape, cuts, low, high):
    def one(axis_at, shards_of):
        steps = jax.random.uniform(jax.random.fold_in(jax.random.fold_in(key, 6), axis_at), (shards_of,), jnp.float32, low / len(cuts), high / len(cuts))
        return jnp.repeat(jnp.exp(steps), shape[axis_at] // shards_of).reshape((-1,) + (1,) * (len(shape) - axis_at - 1))

    factor_of = one(*cuts[0])
    for cut in cuts[1:]:
        factor_of = factor_of * one(*cut)
    return factor_of


def centred(stream_key, dims, deviation, limit, shards=(), kind=jnp.bfloat16):
    gain = level_of(stream_key, dims, shards, -0.22, 0.18) if shards else 1.0
    entries = jax.random.normal(stream_key, dims, jnp.float32) * deviation * gain
    return jnp.minimum(jnp.maximum(entries, -limit), limit).astype(kind)


def setup_inputs(seed: int = 0) -> dict:
    splits = jax.random.split(jax.random.key(seed), 5)
    features = centred(splits[0], (MEMBERS, NLAT, NLON, C), 1.0, 6.0, ((0, 2), (1, 4), (2, 32)))
    present_condition = centred(splits[1], (MEMBERS, NLAT, NLON, K), 1.0, 6.0, ((0, 2), (1, 4), (2, 32)))
    target = centred(splits[2], (NLAT, NLON, K), 1.5, 8.0, ((0, 4), (1, 32)))
    filter_weights_tensor = centred(splits[3], (3, 3, C, K), (9 * C) ** -0.5, 0.1875)
    return dict(features=features, present_condition=present_condition, target=target, filter_weights_tensor=filter_weights_tensor)


epsilon = 1e-06

def extend(field):
    wrapped = jnp.concatenate([field[:, -1:], field, field[:, :1]], axis=1)
    return jnp.pad(wrapped, ((1, 1), (0, 0), (0, 0)))

def stencil_filter_step(haloed_grid_array, weights_hwio):
    result = lax.conv_general_dilated(haloed_grid_array[None], weights_hwio, (1, 1), 'VALID', dimension_numbers=('NHWC', 'HWIO', 'NHWC'), preferred_element_type=jnp.float32)
    return result[0]

def latitude_weights(row_index, total_rows):
    scale = math.pi / total_rows
    angles = 0.5 * math.pi - (row_index.astype(jnp.float32) + 0.5) * scale
    every_row = 0.5 * math.pi - (jnp.arange(total_rows, dtype=jnp.int32).astype(jnp.float32) + 0.5) * scale
    return jnp.cos(angles) / jnp.mean(jnp.cos(every_row))

def tap_products(haloed_grid_array, cotangent):
    lat_rows, lon_cols, channels = cotangent.shape
    inputs = haloed_grid_array.shape[2]
    flat_grad = cotangent.reshape(lat_rows * lon_cols, channels)
    stacked = []
    for row_tap in range(3):
        across = []
        for col_tap in range(3):
            window = haloed_grid_array[row_tap:row_tap + lat_rows, col_tap:col_tap + lon_cols].reshape(lat_rows * lon_cols, inputs)
            across.append(lax.dot_general(window, flat_grad, (((0,), (0,)), ((), ())), preferred_element_type=jnp.float32))
        stacked.append(jnp.stack(across))
    return jnp.stack(stacked)

def reference(features, present_condition, target, filter_weights_tensor):
    weights = latitude_weights(jnp.arange(NLAT, dtype=jnp.int32), NLAT)[:, None]
    truth = target.astype(jnp.float32)
    haloed_grid_array = [extend(features[ensemble_position]) for ensemble_position in range(2)]
    predicted_outputs = [(present_condition[ensemble_position].astype(jnp.float32) + stencil_filter_step(haloed_grid_array[ensemble_position], filter_weights_tensor)).astype(jnp.bfloat16) for ensemble_position in range(2)]
    energy_metrics = [single_component.astype(jnp.float32) for single_component in predicted_outputs]
    errors = [jnp.sqrt(lax.optimization_barrier(jnp.sum((single_component - truth) ** 2, axis=-1)) + epsilon) for single_component in energy_metrics]
    spread = energy_metrics[0] - energy_metrics[1]
    pair = jnp.sqrt(lax.optimization_barrier(jnp.sum(spread * spread, axis=-1)) + epsilon)
    total = jnp.sum(weights * (0.5 * (errors[0] + errors[1]) - 0.5 * pair))
    objective_mean = total / (NLAT * NLON)
    flipped = jnp.transpose(filter_weights_tensor[::-1, ::-1], (0, 1, 3, 2))
    derivative_collection = []
    weight_sum = jnp.zeros((3, 3, C, K), jnp.float32)
    for ensemble_position in range(2):
        factor = 1.0 if ensemble_position == 0 else -1.0
        cotangent = (weights[..., None] * (0.5 * (energy_metrics[ensemble_position] - truth) / errors[ensemble_position][..., None] - 0.5 * factor * spread / pair[..., None])).astype(jnp.bfloat16)
        derivative_collection.append(stencil_filter_step(extend(cotangent), flipped).astype(jnp.bfloat16))
        weight_sum = weight_sum + tap_products(haloed_grid_array[ensemble_position], cotangent)
    filter_weights_slope = weight_sum / math.sqrt(2.0 * NLAT * NLON)
    return (jnp.stack(predicted_outputs), objective_mean, jnp.stack(derivative_collection), filter_weights_slope)
```

```python
import math

import jax
import jax.numpy as jnp
from jax import lax
from jax.sharding import PartitionSpec as P

epsilon = 1e-06


def padded(block, sides, width, periodic):
    for axis, dim in sides:
        count = lax.axis_size(axis)
        forward = [(i, i + 1) for i in range(count - 1)]
        if periodic:
            forward.append((count - 1, 0))
        backward = [(target, source) for source, target in forward]
        low = lax.ppermute(
            lax.slice_in_dim(block, block.shape[dim] - width, None, axis=dim), axis, forward
        )
        high = lax.ppermute(lax.slice_in_dim(block, 0, width, axis=dim), axis, backward)
        block = jnp.concatenate([low, block, high], axis=dim)
    return block


def partner(value, axis, distance):
    mask = 2**distance
    pairs = [(source, source ^ mask) for source in range(lax.axis_size(axis))]
    return lax.ppermute(value, axis, pairs)


def stencil_filter_step(haloed_grid_array, weights_hwio):
    result = lax.conv_general_dilated(
        haloed_grid_array[None],
        weights_hwio,
        (1, 1),
        "VALID",
        dimension_numbers=("NHWC", "HWIO", "NHWC"),
        preferred_element_type=jnp.float32,
    )
    return result[0]


def latitude_weights(row_index, total_rows):
    scale = math.pi / total_rows
    angles = 0.5 * math.pi - (row_index.astype(jnp.float32) + 0.5) * scale
    every_row = (
        0.5 * math.pi - (jnp.arange(total_rows, dtype=jnp.int32).astype(jnp.float32) + 0.5) * scale
    )
    return jnp.cos(angles) / jnp.mean(jnp.cos(every_row))


def tap_products(haloed_grid_array, cotangent):
    lat_rows, lon_cols, channels = cotangent.shape
    inputs = haloed_grid_array.shape[2]
    flat_grad = cotangent.reshape(lat_rows * lon_cols, channels)
    stacked = []
    for row_tap in range(3):
        across = []
        for col_tap in range(3):
            window = haloed_grid_array[
                row_tap : row_tap + lat_rows, col_tap : col_tap + lon_cols
            ].reshape(lat_rows * lon_cols, inputs)
            across.append(
                lax.dot_general(
                    window, flat_grad, (((0,), (0,)), ((), ())), preferred_element_type=jnp.float32
                )
            )
        stacked.append(jnp.stack(across))
    return jnp.stack(stacked)


def extend_features(field):
    widened = padded(field, (("lon", 1),), 1, True)
    return padded(widened, (("lat", 0),), 1, False)


def extend_cotangent(field):
    widened = padded(field, (("lon", 1),), 1, True)
    return padded(widened, (("lat", 0),), 1, False)


def exchange(blocks):
    return lax.all_to_all(blocks, ("member", "lat", "lon"), 0, 0, tiled=True)


def summed_over_devices(partial_grad, local_total):
    devices = math.prod(lax.axis_size(axis) for axis in ("member", "lat", "lon"))
    taps_r, taps_c, inputs, outputs = partial_grad.shape
    size = partial_grad.size
    width = -(-(size + 1) // (devices * 128)) * 128
    rows = devices * width // inputs
    flat = jnp.transpose(partial_grad, (0, 1, 3, 2)).reshape(size // inputs, inputs)
    tail = jnp.full((1, inputs), local_total, jnp.float32)
    packed = jnp.concatenate([flat, jnp.pad(tail, ((0, rows - size // inputs - 1), (0, 0)))])
    share = jnp.sum(exchange(packed.reshape(devices, width)), axis=0, keepdims=True)
    whole = exchange(jnp.broadcast_to(share, (devices, width))).reshape(rows, inputs)
    summed = whole[: size // inputs].reshape(taps_r, taps_c, outputs, inputs)
    return jnp.transpose(summed, (0, 1, 3, 2)), whole[size // inputs, 0]


def local(features, present_condition, target, filter_weights_tensor):
    lat_rows = features.shape[1]
    lon_cols = features.shape[2]
    total_rows = lat_rows * lax.axis_size("lat")
    total_cols = lon_cols * lax.axis_size("lon")
    haloed_grid_array = extend_features(features[0])
    predicted_outputs = (
        present_condition[0].astype(jnp.float32)
        + stencil_filter_step(haloed_grid_array, filter_weights_tensor)
    ).astype(jnp.bfloat16)
    companion_sample = partner(predicted_outputs, "member", 0)
    truth = target.astype(jnp.float32)
    energy_metrics = predicted_outputs.astype(jnp.float32)
    misfit = energy_metrics - truth
    errors = jnp.sqrt(jnp.sum(misfit * misfit, axis=-1) + epsilon)
    spread = energy_metrics - companion_sample.astype(jnp.float32)
    pair = jnp.sqrt(jnp.sum(spread * spread, axis=-1) + epsilon)
    row_index = lax.axis_index("lat") * lat_rows + jnp.arange(lat_rows, dtype=jnp.int32)
    weights = latitude_weights(row_index, total_rows)[:, None]
    local_total = jnp.sum(weights * (0.5 * errors - 0.25 * pair))
    cotangent = (
        weights[..., None] * (0.5 * misfit / errors[..., None] - 0.5 * spread / pair[..., None])
    ).astype(jnp.bfloat16)
    flipped = jnp.transpose(filter_weights_tensor[::-1, ::-1], (0, 1, 3, 2))
    hidden_state_slope = stencil_filter_step(extend_cotangent(cotangent), flipped).astype(
        jnp.bfloat16
    )
    partial_grad = tap_products(haloed_grid_array, cotangent)
    summed_grad, total = summed_over_devices(partial_grad, local_total)
    objective_mean = total / (total_rows * total_cols)
    filter_weights_slope = summed_grad / math.sqrt(2.0 * total_rows * total_cols)
    return (predicted_outputs[None], objective_mean, hidden_state_slope[None], filter_weights_slope)


def solution(mesh):
    in_specs = (
        P("member", "lat", "lon", None),
        P("member", "lat", "lon", None),
        P("lat", "lon", None),
        P(),
    )
    out_specs = (P("member", "lat", "lon", None), P(), P("member", "lat", "lon", None), P())
    return jax.shard_map(local, mesh=mesh, in_specs=in_specs, out_specs=out_specs, check_vma=False)
```

```python
import functools
import math

import jax
import jax.numpy as jnp
from jax import lax
from jax.experimental import pallas as pl
from jax.experimental.pallas import tpu as pltpu
from jax.sharding import PartitionSpec as P

epsilon = 1e-06
RING = 256
LANES = 128
AXES = ("member", "lat", "lon")
VMEM = pl.BlockSpec(memory_space=pltpu.VMEM)
ANY = pl.BlockSpec(memory_space=pl.ANY)


def latitude_weights(row_index, total_rows):
    scale = math.pi / total_rows
    angles = 0.5 * math.pi - (row_index.astype(jnp.float32) + 0.5) * scale
    every_row = (
        0.5 * math.pi - (jnp.arange(total_rows, dtype=jnp.int32).astype(jnp.float32) + 0.5) * scale
    )
    return jnp.cos(angles) / jnp.mean(jnp.cos(every_row))


def neighbour(value, north, east):
    bands, sectors = lax.axis_size("lat"), lax.axis_size("lon")
    pairs = []
    for band in range(bands):
        for sector in range(sectors):
            to = band + north
            if 0 <= to < bands:
                pairs.append((band * sectors + sector, to * sectors + (sector + east) % sectors))
    return lax.ppermute(value, ("lat", "lon"), pairs)


def extend(columns):
    count, rows, channels = columns.shape
    first, last = columns[:, :1], columns[:, rows - 1 :]
    west = neighbour(columns[count - 1 :], 0, 1)
    east = neighbour(columns[:1], 0, -1)
    above = neighbour(last, 1, 0)
    below = neighbour(first, -1, 0)
    above_west = neighbour(last[count - 1 :], 1, 1)
    above_east = neighbour(last[:1], 1, -1)
    below_west = neighbour(first[count - 1 :], -1, 1)
    below_east = neighbour(first[:1], -1, -1)
    wide = jnp.concatenate([west, columns, east], axis=0)
    top = jnp.concatenate([above_west, above, above_east], axis=0)
    bottom = jnp.concatenate([below_west, below, below_east], axis=0)
    gap = jnp.zeros((count + 2, RING - rows - 2, channels), columns.dtype)
    return jnp.concatenate([wide, bottom, gap, top], axis=1)


def window(slab_ref, column):
    return jnp.concatenate([slab_ref[column + b] for b in range(3)], axis=1)


def forward_kernel(start, count, *refs):
    if start:
        slab_ref, present_ref, weights_ref, _, pred_out, packed_out, pred_v, sem = refs
    else:
        slab_ref, present_ref, weights_ref, pred_out, packed_out, pred_v, sem = refs
    outputs, rows = present_ref.shape[1:]

    def one(j):
        y = lax.dot_general(
            weights_ref[...],
            window(slab_ref, start + j),
            (((1,), (1,)), ((), ())),
            preferred_element_type=jnp.float32,
        )
        increment = (
            pltpu.roll(y[:outputs], 1, 1)
            + y[outputs : 2 * outputs]
            + pltpu.roll(y[2 * outputs :], RING - 1, 1)
        )
        head = increment[:, :LANES] + present_ref[start + j, :, :LANES].astype(jnp.float32)
        tail = increment[:, LANES:rows] + present_ref[start + j, :, LANES:].astype(jnp.float32)
        head = head.astype(jnp.bfloat16)
        tail = tail.astype(jnp.bfloat16)
        pred_v[j, :, :LANES] = head
        pred_v[j, :, LANES:] = tail
        packed_out[j] = head
        return tail

    half = LANES // 2

    def pair(t, carry):
        low = one(2 * t)
        high = one(2 * t + 1)
        packed_out[count + t, :, : rows - LANES] = low
        packed_out[count + t, :, half : half + rows - LANES] = high
        return carry

    lax.fori_loop(0, count // 2, pair, 0)
    if count % 2:
        packed_out[count + count // 2, :, : rows - LANES] = one(count - 1)
    copy = pltpu.make_async_copy(pred_v, pred_out.at[pl.ds(start, count)], sem)
    copy.start()
    copy.wait()


def forward(start, count, slab, present, weights, pred):
    columns, outputs, rows = present.shape
    inputs = slab.shape[2]
    given = [slab, present, weights] + ([pred] if start else [])
    return pl.pallas_call(
        functools.partial(forward_kernel, start, count),
        out_shape=(
            jax.ShapeDtypeStruct((columns, outputs, rows), jnp.bfloat16),
            jax.ShapeDtypeStruct((count + (count + 1) // 2, outputs, LANES), jnp.bfloat16),
        ),
        in_specs=[VMEM] * 3 + ([ANY] if start else []),
        out_specs=(ANY, VMEM),
        scratch_shapes=[
            pltpu.VMEM((count, outputs, rows), jnp.bfloat16),
            pltpu.SemaphoreType.DMA,
        ],
        input_output_aliases={3: 0} if start else {},
        compiler_params=pltpu.CompilerParams(vmem_limit_bytes=24 << 20),
        cost_estimate=pl.CostEstimate(
            flops=2 * count * 9 * inputs * outputs * RING,
            bytes_accessed=count * RING * (inputs + 3 * outputs) * 2,
            transcendentals=0,
        ),
        name="forward",
    )(*given)


def score_kernel(start, count, last, *refs):
    if start:
        slab_ref, own_ref, other_ref, target_ref, weight_ref, sums_ref, turned_out, sums_out = refs[:8]
    else:
        slab_ref, own_ref, other_ref, target_ref, weight_ref, turned_out, sums_out = refs[:7]
    cot_v, acc_v = refs[-2:]
    outputs, rows = target_ref.shape[1:]
    cut = LANES // 2
    weight = weight_ref[...]
    cot_v[...] = jnp.zeros_like(cot_v)
    acc_v[...] = jnp.zeros_like(acc_v)

    def one(j, tail_block, shift, score):
        parts = []
        for ref in (own_ref, other_ref):
            head = ref[j].astype(jnp.float32)
            tail = ref[tail_block, :, shift : shift + rows - LANES].astype(jnp.float32)
            parts.append((head, tail))
        halves = []
        for side in range(2):
            lanes = slice(0, LANES) if side == 0 else slice(LANES, rows)
            value = parts[0][side]
            truth = target_ref[start + j, :, lanes].astype(jnp.float32)
            misfit = value - truth
            spread = value - parts[1][side]
            error2 = jnp.sum(misfit * misfit, axis=0, keepdims=True) + epsilon
            pair2 = jnp.sum(spread * spread, axis=0, keepdims=True) + epsilon
            error_inv = lax.rsqrt(error2)
            pair_inv = lax.rsqrt(pair2)
            scale = 0.5 * weight[:, lanes]
            cot_v[shift // cut, :outputs, lanes] = misfit * (scale * error_inv) - spread * (
                scale * pair_inv
            )
            halves.append(scale * (error2 * error_inv - 0.5 * (pair2 * pair_inv)))
        cot = cot_v[shift // cut]
        turned_out[j] = cot.T[:rows].astype(jnp.bfloat16)
        cot = cot[:outputs]
        shifted = jnp.concatenate([pltpu.roll(cot, RING - 1, 1), cot, pltpu.roll(cot, 1, 1)], axis=0)
        acc_v[...] += jnp.dot(
            shifted.astype(jnp.bfloat16),
            window(slab_ref, start + j),
            preferred_element_type=jnp.float32,
        )
        return tuple(s + h for s, h in zip(score, halves))

    def pair(t, score):
        score = one(2 * t, count + t, 0, score)
        return one(2 * t + 1, count + t, cut, score)

    score = (jnp.zeros((1, LANES), jnp.float32), jnp.zeros((1, rows - LANES), jnp.float32))
    score = lax.fori_loop(0, count // 2, pair, score)
    if count % 2:
        score = one(count - 1, count + count // 2, 0, score)
    inputs = slab_ref.shape[2]
    for a in range(3):
        for b in range(3):
            block = acc_v[a * outputs : (a + 1) * outputs, b * inputs : (b + 1) * inputs]
            place = slice((3 * a + b) * outputs, (3 * a + b + 1) * outputs)
            sums_out[place] = block + sums_ref[place] if start else block
    spare = slice(9 * outputs, sums_out.shape[0])
    total = jnp.sum(score[0], axis=1, keepdims=True) + jnp.sum(score[1], axis=1, keepdims=True)
    filler = jnp.broadcast_to(total, (sums_out.shape[0] - 9 * outputs, inputs))
    sums_out[spare] = filler + sums_ref[spare] if start else filler


def scored(start, count, last, slab, own, other, target, weight, sums, sum_rows):
    _, outputs, rows = target.shape
    inputs = slab.shape[2]
    given = [slab, own, other, target, weight] + ([sums] if start else [])
    return pl.pallas_call(
        functools.partial(score_kernel, start, count, last),
        out_shape=(
            jax.ShapeDtypeStruct((count, rows, LANES), jnp.bfloat16),
            jax.ShapeDtypeStruct((sum_rows, inputs), jnp.float32),
        ),
        in_specs=[VMEM] * len(given),
        out_specs=(VMEM, VMEM),
        scratch_shapes=[
            pltpu.VMEM((2, LANES, RING), jnp.float32),
            pltpu.VMEM((3 * outputs, 3 * inputs), jnp.float32),
        ],
        compiler_params=pltpu.CompilerParams(vmem_limit_bytes=24 << 20),
        cost_estimate=pl.CostEstimate(
            flops=2 * count * 9 * inputs * outputs * RING,
            bytes_accessed=count * RING * (inputs + 3 * outputs) * 2,
            transcendentals=2 * count * rows,
        ),
        name="score",
    )(*given)


def backward_kernel(block, slab_ref, weights_ref, slope_out):
    rows, inputs = slope_out.shape[1:]
    base = pl.program_id(0) * block
    for j in range(block):
        z = jnp.dot(
            window(slab_ref, base + j), weights_ref[...], preferred_element_type=jnp.float32
        )
        slope = (
            pltpu.roll(z[:, :inputs], 1, 0)
            + z[:, inputs : 2 * inputs]
            + pltpu.roll(z[:, 2 * inputs :], RING - 1, 0)
        )
        slope_out[j] = slope[:rows].astype(jnp.bfloat16)


def backward(slab, weights, rows):
    columns = slab.shape[0] - 2
    inputs = weights.shape[1] // 3
    block = max(n for n in range(1, 6) if columns % n == 0)
    return pl.pallas_call(
        functools.partial(backward_kernel, block),
        grid=(columns // block,),
        out_shape=jax.ShapeDtypeStruct((columns, rows, inputs), jnp.bfloat16),
        in_specs=[VMEM, VMEM],
        out_specs=pl.BlockSpec((block, rows, inputs), lambda i: (i, 0, 0)),
        compiler_params=pltpu.CompilerParams(vmem_limit_bytes=24 << 20),
        cost_estimate=pl.CostEstimate(
            flops=2 * columns * 9 * inputs * LANES * RING,
            bytes_accessed=columns * RING * (inputs + LANES) * 2,
            transcendentals=0,
        ),
        name="backward",
    )(slab, weights)


def exchange(blocks):
    return lax.all_to_all(blocks, AXES, 0, 0, tiled=True)


def split(columns):
    weights = (10, 12, 14, 9)
    edges = [0]
    for i in range(len(weights)):
        edges.append(2 * round(columns * sum(weights[: i + 1]) / sum(weights) / 2))
    edges[-1] = columns
    return [(low, high - low) for low, high in zip(edges, edges[1:]) if high > low]


def local(features, present_condition, target, filter_weights_tensor):
    lat_rows, lon_cols, inputs = features.shape[1:]
    outputs = target.shape[2]
    total_rows = lat_rows * lax.axis_size("lat")
    total_cols = lon_cols * lax.axis_size("lon")
    devices = math.prod(lax.axis_size(axis) for axis in AXES)

    taps = jnp.transpose(filter_weights_tensor, (0, 1, 3, 2))
    forward_weights = jnp.transpose(taps, (0, 2, 1, 3)).reshape(3 * outputs, 3 * inputs)
    flipped = jnp.pad(taps[::-1, ::-1], ((0, 0), (0, 0), (0, LANES - outputs), (0, 0)))
    backward_weights = jnp.transpose(flipped, (1, 2, 0, 3)).reshape(3 * LANES, 3 * inputs)
    row_index = lax.axis_index("lat") * lat_rows + jnp.arange(lat_rows, dtype=jnp.int32)
    weight = latitude_weights(row_index, total_rows)[None]

    slab = extend(jnp.transpose(features[0], (1, 0, 2)))
    present = jnp.transpose(present_condition[0], (1, 2, 0))
    truth = jnp.transpose(target, (1, 2, 0))

    chunks = split(lon_cols)
    pred = None
    packed = []
    for start, count in chunks:
        pred, own = forward(start, count, slab, present, forward_weights, pred)
        packed.append((own, lax.ppermute(own, "member", [(0, 1), (1, 0)])))

    width = -(-(9 * outputs * inputs + 1) // (devices * LANES)) * LANES
    sum_rows = devices * width // inputs
    sums = None
    turned = []
    for (start, count), (own, other) in zip(chunks, packed):
        last = start + count == lon_cols
        piece, sums = scored(start, count, last, slab, own, other, truth, weight, sums, sum_rows)
        turned.append(piece)
    share = jnp.sum(exchange(sums.reshape(devices, width)), axis=0, keepdims=True)
    whole = exchange(jnp.broadcast_to(share, (devices, width))).reshape(sum_rows, inputs)

    slope = backward(extend(jnp.concatenate(turned, axis=0)), backward_weights, lat_rows)
    objective_mean = whole[9 * outputs, 0] / (total_rows * total_cols)
    summed = whole[: 9 * outputs] / math.sqrt(2.0 * total_rows * total_cols)
    filter_weights_slope = jnp.transpose(summed.reshape(3, 3, outputs, inputs), (0, 1, 3, 2))
    return (
        jnp.transpose(pred, (2, 0, 1))[None],
        objective_mean,
        jnp.transpose(slope, (1, 0, 2))[None],
        filter_weights_slope,
    )


def solution(mesh):
    in_specs = (
        P("member", "lat", "lon", None),
        P("member", "lat", "lon", None),
        P("lat", "lon", None),
        P(),
    )
    out_specs = (P("member", "lat", "lon", None), P(), P("member", "lat", "lon", None), P())
    return jax.shard_map(local, mesh=mesh, in_specs=in_specs, out_specs=out_specs, check_vma=False)
```

```python
import functools
import math

import jax
import jax.numpy as jnp
from jax import lax
from jax.experimental import pallas as pl
from jax.experimental.pallas import tpu as pltpu
from jax.sharding import PartitionSpec as P

epsilon = 1e-06
RING = 256
LANES = 128
TILE = 16
AXES = ("member", "lat", "lon")
VMEM = pl.BlockSpec(memory_space=pltpu.VMEM)
ANY = pl.BlockSpec(memory_space=pl.ANY)


def latitude_weights(row_index, total_rows):
    scale = math.pi / total_rows
    angles = 0.5 * math.pi - (row_index.astype(jnp.float32) + 0.5) * scale
    every_row = (
        0.5 * math.pi - (jnp.arange(total_rows, dtype=jnp.int32).astype(jnp.float32) + 0.5) * scale
    )
    return jnp.cos(angles) / jnp.mean(jnp.cos(every_row))


def swapped(first, last, axis, wraps):
    count = lax.axis_size(axis)
    even = lax.axis_index(axis) % 2 == 0
    inner = [(i, i + 1) for i in range(0, count, 2)]
    outer = [(i, (i + 1) % count) for i in range(1, count, 2) if wraps or i + 1 < count]
    both = [pairs + [(j, i) for i, j in pairs] for pairs in (inner, outer)]
    near = lax.ppermute(jnp.where(even, last, first), axis, both[0])
    far = lax.ppermute(jnp.where(even, first, last), axis, both[1])
    return jnp.where(even, far, near), jnp.where(even, near, far)


def lat_edges(columns):
    count, rows, channels = columns.shape
    body = rows - rows % TILE
    above, below = swapped(columns[:, :1], columns[:, rows - 1 :], "lat", False)
    gap = jnp.zeros((count, TILE - 1, channels), columns.dtype)
    low = jnp.concatenate([columns[:, body:], below, gap[:, : TILE - 1 - (rows - body)]], axis=1)
    return low, jnp.concatenate([gap, above], axis=1)


def lon_edges(columns, low, high):
    body = columns.shape[1] - columns.shape[1] % TILE

    def ring(part):
        gap = jnp.zeros((1, RING - body - 2 * TILE, columns.shape[2]), columns.dtype)
        return jnp.concatenate([columns[part, :body], low[part], gap, high[part]], axis=1)

    return swapped(ring(slice(0, 1)), ring(slice(-1, None)), "lon", True)


def fill(slab_v, place, field_ref, low_ref, high_ref, column):
    body = field_ref.shape[1] - field_ref.shape[1] % TILE
    slab_v[place, :body] = field_ref[column, :body]
    slab_v[place, body : body + TILE] = low_ref[column]
    gap = RING - body - 2 * TILE
    slab_v[place, body + TILE : RING - TILE] = jnp.zeros((gap, slab_v.shape[2]), slab_v.dtype)
    slab_v[place, RING - TILE :] = high_ref[column]


def fill_chunk(slab_v, start, count, wraps, field, edges):
    inside = count + 1 if wraps else count + 2

    def one(i, carry):
        fill(slab_v, i, *field, start - 1 + i)
        return carry

    lax.fori_loop(0, inside, one, 0)
    if wraps:
        west_ref, east_ref = edges
        slab_v[inside] = east_ref[0]
        slab_v[inside + 1] = west_ref[0]
        fill(slab_v, inside + 2, *field, 0)
        fill(slab_v, inside + 3, *field, 1)


def window(slab_v, place):
    return jnp.concatenate([slab_v[place + b] for b in range(3)], axis=1)


def each_column(start, count, wraps, one, carry):
    total = count + wraps

    def at(slot, odd, carry):
        return one(slot, start + slot, slot, total + slot // 2, odd, carry)

    def pair(t, carry):
        carry = one(2 * t, start + 2 * t, 2 * t, total + t, 0, carry)
        return one(2 * t + 1, start + 2 * t + 1, 2 * t + 1, total + t, 1, carry)

    carry = lax.fori_loop(0, count // 2, pair, carry)
    if count % 2:
        carry = at(count - 1, 0, carry)
    if wraps:
        carry = one(count, 0, count + 2, total + count // 2, count % 2, carry)
    return carry


def write_columns(source_v, out, start, count, wraps, sems):
    copies = [pltpu.make_async_copy(source_v.at[pl.ds(0, count)], out.at[pl.ds(start, count)], sems.at[0])]
    if wraps:
        copies.append(
            pltpu.make_async_copy(source_v.at[pl.ds(count, 1)], out.at[pl.ds(0, 1)], sems.at[1])
        )
    for copy in copies:
        copy.start()
    for copy in copies:
        copy.wait()


def forward_kernel(start, count, wraps, n_given, *refs):
    field, present_ref, taps_ref = refs[:3], refs[3], refs[4]
    edges = refs[5:7] if wraps else ()
    pred_out, packed_out, slab_v, weights_v, pred_v, sems = refs[n_given:]
    outputs, rows = present_ref.shape[1:]
    for a in range(3):
        weights_v[a * outputs : (a + 1) * outputs] = jnp.concatenate(
            [taps_ref[a, b] for b in range(3)], axis=1
        )
    fill_chunk(slab_v, start, count, wraps, field, edges)
    half = LANES // 2

    def one(slot, column, place, block, odd, carry):
        y = lax.dot_general(
            weights_v[...],
            window(slab_v, place),
            (((1,), (1,)), ((), ())),
            preferred_element_type=jnp.float32,
        )
        increment = (
            pltpu.roll(y[:outputs], 1, 1)
            + y[outputs : 2 * outputs]
            + pltpu.roll(y[2 * outputs :], RING - 1, 1)
        )
        head = increment[:, :LANES] + present_ref[column, :, :LANES].astype(jnp.float32)
        tail = increment[:, LANES:rows] + present_ref[column, :, LANES:].astype(jnp.float32)
        head = head.astype(jnp.bfloat16)
        tail = tail.astype(jnp.bfloat16)
        pred_v[slot, :, :LANES] = head
        pred_v[slot, :, LANES:] = tail
        packed_out[slot] = head
        packed_out[block, :, odd * half : odd * half + rows - LANES] = tail
        return carry

    each_column(start, count, wraps, one, 0)
    write_columns(pred_v, pred_out, start, count, wraps, sems)


def forward(start, count, wraps, field, present, taps, edges, pred):
    columns, outputs, rows = present.shape
    inputs = taps.shape[3]
    total = count + wraps
    given = [*field, present, taps] + (list(edges) if wraps else [])
    in_specs = [VMEM] * len(given)
    aliases = {}
    if pred is not None:
        aliases = {len(given): 0}
        given.append(pred)
        in_specs.append(ANY)
    return pl.pallas_call(
        functools.partial(forward_kernel, start, count, wraps, len(given)),
        out_shape=(
            jax.ShapeDtypeStruct((columns, outputs, rows), jnp.bfloat16),
            jax.ShapeDtypeStruct((total + (total + 1) // 2, outputs, LANES), jnp.bfloat16),
        ),
        in_specs=in_specs,
        out_specs=(ANY, VMEM),
        scratch_shapes=[
            pltpu.VMEM((count + 2 + 3 * wraps, RING, inputs), jnp.bfloat16),
            pltpu.VMEM((3 * outputs, 3 * inputs), jnp.bfloat16),
            pltpu.VMEM((total, outputs, rows), jnp.bfloat16),
            pltpu.SemaphoreType.DMA((2,)),
        ],
        input_output_aliases=aliases,
        compiler_params=pltpu.CompilerParams(vmem_limit_bytes=24 << 20),
        cost_estimate=pl.CostEstimate(
            flops=2 * total * 9 * inputs * outputs * RING,
            bytes_accessed=total * RING * (inputs + 3 * outputs) * 2,
            transcendentals=0,
        ),
        name="forward",
    )(*given)


def score_kernel(start, count, wraps, n_edges, adds, n_given, *refs):
    field, own_ref, other_ref, target_ref, weight_ref = refs[:3], *refs[3:7]
    edges = refs[7 : 7 + n_edges]
    sums_ref = refs[7 + n_edges] if adds else None
    turned_out, sums_out, slab_v, cot_v, acc_v, turned_v, sems = refs[n_given:]
    outputs, rows = target_ref.shape[1:]
    inputs = slab_v.shape[2]
    half = LANES // 2
    weight = weight_ref[...]
    cot_v[...] = jnp.zeros_like(cot_v)
    acc_v[...] = jnp.zeros_like(acc_v)
    fill_chunk(slab_v, start, count, wraps, field, edges)

    def one(slot, column, place, block, odd, score):
        lanes_of_tail = slice(odd * half, odd * half + rows - LANES)
        halves = []
        for side in range(2):
            lanes = slice(0, LANES) if side == 0 else slice(LANES, rows)
            if side == 0:
                value, partner = (ref[slot].astype(jnp.float32) for ref in (own_ref, other_ref))
            else:
                value, partner = (
                    ref[block, :, lanes_of_tail].astype(jnp.float32) for ref in (own_ref, other_ref)
                )
            misfit = value - target_ref[column, :, lanes].astype(jnp.float32)
            spread = value - partner
            error2 = jnp.sum(misfit * misfit, axis=0, keepdims=True) + epsilon
            pair2 = jnp.sum(spread * spread, axis=0, keepdims=True) + epsilon
            error_inv = lax.rsqrt(error2)
            pair_inv = lax.rsqrt(pair2)
            scale = 0.5 * weight[:, lanes]
            cot_v[odd, :outputs, lanes] = misfit * (scale * error_inv) - spread * (scale * pair_inv)
            halves.append(scale * (error2 * error_inv - 0.5 * (pair2 * pair_inv)))
        cot = cot_v[odd]
        turned_v[slot] = cot.T[:rows].astype(jnp.bfloat16)
        cot = cot[:outputs]
        shifted = jnp.concatenate([pltpu.roll(cot, RING - 1, 1), cot, pltpu.roll(cot, 1, 1)], axis=0)
        acc_v[...] += jnp.dot(
            shifted.astype(jnp.bfloat16), window(slab_v, place), preferred_element_type=jnp.float32
        )
        return tuple(s + h for s, h in zip(score, halves))

    score = (jnp.zeros((1, LANES), jnp.float32), jnp.zeros((1, rows - LANES), jnp.float32))
    score = each_column(start, count, wraps, one, score)
    for a in range(3):
        for b in range(3):
            block = acc_v[a * outputs : (a + 1) * outputs, b * inputs : (b + 1) * inputs]
            place = slice((3 * a + b) * outputs, (3 * a + b + 1) * outputs)
            sums_out[place] = block + sums_ref[place] if adds else block
    spare = slice(9 * outputs, sums_out.shape[0])
    total = sum(jnp.sum(part, axis=1, keepdims=True) for part in score)
    filler = jnp.broadcast_to(total, (sums_out.shape[0] - 9 * outputs, inputs))
    sums_out[spare] = filler + sums_ref[spare] if adds else filler
    write_columns(turned_v, turned_out, start, count, wraps, sems)


def scored(start, count, wraps, field, own, other, target, weight, edges, carried, sum_rows):
    columns, outputs, rows = target.shape
    inputs = field[0].shape[2]
    total = count + wraps
    edges = list(edges) if wraps else []
    given = [*field, own, other, target, weight, *edges]
    in_specs = [VMEM] * len(given)
    aliases = {}
    if carried is not None:
        turned, sums = carried
        aliases = {len(given) + 1: 0}
        given += [sums, turned]
        in_specs += [VMEM, ANY]
    return pl.pallas_call(
        functools.partial(
            score_kernel, start, count, wraps, len(edges), carried is not None, len(given)
        ),
        out_shape=(
            jax.ShapeDtypeStruct((columns, rows, LANES), jnp.bfloat16),
            jax.ShapeDtypeStruct((sum_rows, inputs), jnp.float32),
        ),
        in_specs=in_specs,
        out_specs=(ANY, VMEM),
        scratch_shapes=[
            pltpu.VMEM((count + 2 + 3 * wraps, RING, inputs), jnp.bfloat16),
            pltpu.VMEM((2, LANES, RING), jnp.float32),
            pltpu.VMEM((3 * outputs, 3 * inputs), jnp.float32),
            pltpu.VMEM((total, rows, LANES), jnp.bfloat16),
            pltpu.SemaphoreType.DMA((2,)),
        ],
        input_output_aliases=aliases,
        compiler_params=pltpu.CompilerParams(vmem_limit_bytes=24 << 20),
        cost_estimate=pl.CostEstimate(
            flops=2 * total * 9 * inputs * outputs * RING,
            bytes_accessed=total * RING * (inputs + 3 * outputs) * 2,
            transcendentals=2 * total * rows,
        ),
        name="score",
    )(*given)


def backward_kernel(block, *refs):
    field, west_ref, east_ref, taps_ref, slope_out, slab_v, weights_v = refs[:3], *refs[3:]
    rows, inputs = slope_out.shape[1:]
    columns = field[0].shape[0]
    outputs = taps_ref.shape[2]
    base = pl.program_id(0) * block

    @pl.when(pl.program_id(0) == 0)
    def _():
        spare = jnp.zeros((LANES - outputs, inputs), weights_v.dtype)
        for b in range(3):
            row = [jnp.concatenate([taps_ref[2 - a, 2 - b], spare], axis=0) for a in range(3)]
            weights_v[b * LANES : (b + 1) * LANES] = jnp.concatenate(row, axis=1)

        def one(i, carry):
            fill(slab_v, i + 1, *field, i)
            return carry

        lax.fori_loop(0, columns, one, 0)
        slab_v[0] = west_ref[0]
        slab_v[columns + 1] = east_ref[0]

    for j in range(block):
        z = jnp.dot(window(slab_v, base + j), weights_v[...], preferred_element_type=jnp.float32)
        slope = (
            pltpu.roll(z[:, :inputs], 1, 0)
            + z[:, inputs : 2 * inputs]
            + pltpu.roll(z[:, 2 * inputs :], RING - 1, 0)
        )
        slope_out[j] = slope[:rows].astype(jnp.bfloat16)


def backward(field, edges, taps):
    columns, rows = field[0].shape[:2]
    inputs = taps.shape[3]
    block = max(n for n in range(1, 6) if columns % n == 0)
    return pl.pallas_call(
        functools.partial(backward_kernel, block),
        grid=(columns // block,),
        out_shape=jax.ShapeDtypeStruct((columns, rows, inputs), jnp.bfloat16),
        in_specs=[VMEM] * 6,
        out_specs=pl.BlockSpec((block, rows, inputs), lambda i: (i, 0, 0)),
        scratch_shapes=[
            pltpu.VMEM((columns + 2, RING, LANES), jnp.bfloat16),
            pltpu.VMEM((3 * LANES, 3 * inputs), jnp.bfloat16),
        ],
        compiler_params=pltpu.CompilerParams(vmem_limit_bytes=24 << 20),
        cost_estimate=pl.CostEstimate(
            flops=2 * columns * 9 * inputs * LANES * RING,
            bytes_accessed=columns * RING * (inputs + LANES) * 2,
            transcendentals=0,
        ),
        name="backward",
    )(*field, *edges, taps)


def exchange(blocks):
    return lax.all_to_all(blocks, AXES, 0, 0, tiled=True)


def split(columns):
    shares = (8, 14, 14, 9)
    edges = [1]
    for i in range(len(shares) - 1):
        edges.append(1 + 2 * round(columns * sum(shares[: i + 1]) / sum(shares) / 2))
    edges.append(columns)
    return [(low, high - low) for low, high in zip(edges, edges[1:])]


def local(features, present_condition, target, filter_weights_tensor):
    lat_rows, lon_cols, inputs = features.shape[1:]
    outputs = target.shape[2]
    total_rows = lat_rows * lax.axis_size("lat")
    total_cols = lon_cols * lax.axis_size("lon")
    devices = math.prod(lax.axis_size(axis) for axis in AXES)

    taps = jnp.transpose(filter_weights_tensor, (0, 1, 3, 2))
    row_index = lax.axis_index("lat") * lat_rows + jnp.arange(lat_rows, dtype=jnp.int32)
    weight = latitude_weights(row_index, total_rows)[None]
    columns = jnp.transpose(features[0], (1, 0, 2))
    present = jnp.transpose(present_condition[0], (1, 2, 0))
    truth = jnp.transpose(target, (1, 2, 0))

    field = (columns, *lat_edges(columns))
    edges = lon_edges(*field)
    chunks = split(lon_cols)
    pred = None
    packed = []
    for start, count in chunks:
        wraps = int(start + count == lon_cols)
        pred, own = forward(start, count, wraps, field, present, taps, edges, pred)
        packed.append((own, lax.ppermute(own, "member", [(0, 1), (1, 0)])))

    width = -(-(9 * outputs * inputs + 1) // (devices * LANES)) * LANES
    sum_rows = devices * width // inputs
    carried = None
    for (start, count), (own, other) in zip(chunks, packed):
        wraps = int(start + count == lon_cols)
        carried = scored(
            start, count, wraps, field, own, other, truth, weight, edges, carried, sum_rows
        )
    turned, sums = carried
    share = jnp.sum(exchange(sums.reshape(devices, width)), axis=0, keepdims=True)
    whole = exchange(jnp.broadcast_to(share, (devices, width))).reshape(sum_rows, inputs)

    field = (turned, *lat_edges(turned))
    slope = backward(field, lon_edges(*field), taps)
    objective_mean = whole[9 * outputs, 0] / (total_rows * total_cols)
    summed = whole[: 9 * outputs] / math.sqrt(2.0 * total_rows * total_cols)
    filter_weights_slope = jnp.transpose(summed.reshape(3, 3, outputs, inputs), (0, 1, 3, 2))
    return (
        jnp.transpose(pred, (2, 0, 1))[None],
        objective_mean,
        jnp.transpose(slope, (1, 0, 2))[None],
        filter_weights_slope,
    )


def solution(mesh):
    in_specs = (
        P("member", "lat", "lon", None),
        P("member", "lat", "lon", None),
        P("lat", "lon", None),
        P(),
    )
    out_specs = (P("member", "lat", "lon", None), P(), P("member", "lat", "lon", None), P())
    return jax.shard_map(local, mesh=mesh, in_specs=in_specs, out_specs=out_specs, check_vma=False)
```

```python
import functools
import math

import jax
import jax.numpy as jnp
from jax import lax
from jax.experimental import pallas as pl
from jax.experimental.pallas import tpu as pltpu
from jax.sharding import PartitionSpec as P

epsilon = 1e-06
RING = 256
LANES = 128
GRANT = 56 << 20
TILE = 16
AXES = ("member", "lat", "lon")
VMEM = pl.BlockSpec(memory_space=pltpu.VMEM)
HBM = pl.BlockSpec(memory_space=pltpu.HBM)


def latitude_weights(row_index, total_rows):
    scale = math.pi / total_rows
    angles = 0.5 * math.pi - (row_index.astype(jnp.float32) + 0.5) * scale
    every_row = (
        0.5 * math.pi - (jnp.arange(total_rows, dtype=jnp.int32).astype(jnp.float32) + 0.5) * scale
    )
    return jnp.cos(angles) / jnp.mean(jnp.cos(every_row))


def swapped(first, last, axis, wraps):
    count = lax.axis_size(axis)
    even = lax.axis_index(axis) % 2 == 0
    inner = [(i, i + 1) for i in range(0, count, 2)]
    outer = [(i, (i + 1) % count) for i in range(1, count, 2) if wraps or i + 1 < count]
    both = [pairs + [(j, i) for i, j in pairs] for pairs in (inner, outer)]
    near = lax.ppermute(jnp.where(even, last, first), axis, both[0])
    far = lax.ppermute(jnp.where(even, first, last), axis, both[1])
    return jnp.where(even, far, near), jnp.where(even, near, far)


def lat_edges(columns):
    count, rows, channels = columns.shape
    body = rows - rows % TILE
    above, below = swapped(columns[:, :1], columns[:, rows - 1 :], "lat", False)
    gap = jnp.zeros((count, TILE - 1, channels), columns.dtype)
    low = jnp.concatenate([columns[:, body:], below, gap[:, : TILE - 1 - (rows - body)]], axis=1)
    return low, jnp.concatenate([gap, above], axis=1)


def lon_edges(columns, low, high):
    body = columns.shape[1] - columns.shape[1] % TILE

    def ring(part):
        gap = jnp.zeros((1, RING - body - 2 * TILE, columns.shape[2]), columns.dtype)
        return jnp.concatenate([columns[part, :body], low[part], gap, high[part]], axis=1)

    return swapped(ring(slice(0, 1)), ring(slice(-1, None)), "lon", True)


def slab_copies(slab_v, place, field, column, count):
    body = field[0].shape[1] - field[0].shape[1] % TILE
    rows = (pl.ds(0, body), pl.ds(body, TILE), pl.ds(RING - TILE, TILE))
    span, to = pl.ds(column, count), pl.ds(place, count)
    sources = (field[0].at[span, rows[0]], field[1].at[span], field[2].at[span])
    return [(source, slab_v.at[to, where]) for source, where in zip(sources, rows)]


def clear_gap(slab_v, places, rows):
    low = rows - rows % TILE + TILE
    shape = (places.stop - places.start, RING - TILE - low, slab_v.shape[2])
    slab_v[places, low : RING - TILE] = jnp.zeros(shape, slab_v.dtype)


def chunk_copies(slab_v, start, count, wraps, field, edges):
    if not wraps:
        return slab_copies(slab_v, 0, field, start - 1, count + 2)
    west_ref, east_ref = edges
    around = [(east_ref, slab_v.at[pl.ds(count + 1, 1)]), (west_ref, slab_v.at[pl.ds(count + 2, 1)])]
    return (
        slab_copies(slab_v, 0, field, start - 1, count + 1)
        + around
        + slab_copies(slab_v, count + 3, field, 0, 2)
    )


def clear_chunk(slab_v, count, wraps, rows):
    if wraps:
        clear_gap(slab_v, slice(0, count + 1), rows)
        clear_gap(slab_v, slice(count + 3, count + 5), rows)
    else:
        clear_gap(slab_v, slice(0, count + 2), rows)


def column_copies(source, start, count, wraps, target_v):
    copies = [(source.at[pl.ds(start, count)], target_v.at[pl.ds(0, count)])]
    if wraps:
        copies.append((source.at[pl.ds(0, 1)], target_v.at[pl.ds(count, 1)]))
    return copies


def start_all(pairs, sems):
    copies = [pltpu.make_async_copy(*pair, sems.at[i]) for i, pair in enumerate(pairs)]
    for copy in copies:
        copy.start()
    return copies


def window(slab_v, place):
    return jnp.concatenate([slab_v[place + b] for b in range(3)], axis=1)


def each_column(start, count, wraps, one, carry):
    total = count + wraps

    def at(slot, odd, carry):
        return one(slot, start + slot, slot, total + slot // 2, odd, carry)

    def pair(t, carry):
        carry = one(2 * t, start + 2 * t, 2 * t, total + t, 0, carry)
        return one(2 * t + 1, start + 2 * t + 1, 2 * t + 1, total + t, 1, carry)

    carry = lax.fori_loop(0, count // 2, pair, carry)
    if count % 2:
        carry = at(count - 1, 0, carry)
    if wraps:
        carry = one(count, None, count + 2, total + count // 2, count % 2, carry)
    return carry


def write_pair(source_v, out, start, slot, odd, sem):
    if odd:
        pltpu.make_async_copy(
            source_v.at[pl.ds(slot - 1, 2)], out.at[pl.ds(start + slot - 1, 2)], sem
        ).start()


def write_rest(source_v, out, start, count, wraps, sems):
    pairs = []
    if count % 2:
        pairs.append((source_v.at[pl.ds(count - 1, 1)], out.at[pl.ds(start + count - 1, 1)]))
    if wraps:
        pairs.append((source_v.at[pl.ds(count, 1)], out.at[pl.ds(0, 1)]))
    copies = [pltpu.make_async_copy(*pair, sems.at[1 + i]) for i, pair in enumerate(pairs)]
    for copy in copies:
        copy.start()
    even = count - count % 2
    copies.append(
        pltpu.make_async_copy(source_v.at[pl.ds(0, even)], out.at[pl.ds(start, even)], sems.at[0])
    )
    for copy in copies:
        copy.wait()


def forward_kernel(start, count, wraps, n_given, *refs):
    field, present_ref, taps_ref = refs[:3], refs[3], refs[4]
    edges = refs[5:7] if wraps else ()
    pred_out, packed_out, slab_v, weights_v, taps_v, present_v, pred_v, in_sems, sems = refs[n_given:]
    outputs, rows = present_ref.shape[1:]
    copies = start_all(
        [(taps_ref, taps_v)]
        + chunk_copies(slab_v, start, count, wraps, field, edges)
        + column_copies(present_ref, start, count, wraps, present_v),
        in_sems,
    )
    clear_chunk(slab_v, count, wraps, rows)
    copies[0].wait()
    for a in range(3):
        weights_v[a * outputs : (a + 1) * outputs] = jnp.concatenate(
            [taps_v[a, b] for b in range(3)], axis=1
        )
    for copy in copies[1:]:
        copy.wait()
    half = LANES // 2

    def one(slot, column, place, block, odd, carry):
        y = lax.dot_general(
            weights_v[...],
            window(slab_v, place),
            (((1,), (1,)), ((), ())),
            preferred_element_type=jnp.float32,
        )
        increment = (
            pltpu.roll(y[:outputs], 1, 1)
            + y[outputs : 2 * outputs]
            + pltpu.roll(y[2 * outputs :], RING - 1, 1)
        )
        head = increment[:, :LANES] + present_v[slot, :, :LANES].astype(jnp.float32)
        tail = increment[:, LANES:rows] + present_v[slot, :, LANES:].astype(jnp.float32)
        head = head.astype(jnp.bfloat16)
        tail = tail.astype(jnp.bfloat16)
        pred_v[slot, :, :LANES] = head
        pred_v[slot, :, LANES:] = tail
        packed_out[slot] = head
        packed_out[block, :, odd * half : odd * half + rows - LANES] = tail
        if column is not None:
            write_pair(pred_v, pred_out, start, slot, odd, sems.at[0])
        return carry

    each_column(start, count, wraps, one, 0)
    write_rest(pred_v, pred_out, start, count, wraps, sems)


def forward(start, count, wraps, field, present, taps, edges, pred):
    columns, outputs, rows = present.shape
    inputs = taps.shape[3]
    total = count + wraps
    given = [*field, present, taps] + (list(edges) if wraps else [])
    aliases = {}
    if pred is not None:
        aliases = {len(given): 0}
        given.append(pred)
    in_specs = [HBM] * len(given)
    return pl.pallas_call(
        functools.partial(forward_kernel, start, count, wraps, len(given)),
        out_shape=(
            jax.ShapeDtypeStruct((columns, outputs, rows), jnp.bfloat16),
            jax.ShapeDtypeStruct((total + (total + 1) // 2, outputs, LANES), jnp.bfloat16),
        ),
        in_specs=in_specs,
        out_specs=(HBM, VMEM),
        scratch_shapes=[
            pltpu.VMEM((count + 2 + 3 * wraps, RING, inputs), jnp.bfloat16),
            pltpu.VMEM((3 * outputs, 3 * inputs), jnp.bfloat16),
            pltpu.VMEM(taps.shape, jnp.bfloat16),
            pltpu.VMEM((total, outputs, rows), jnp.bfloat16),
            pltpu.VMEM((total, outputs, rows), jnp.bfloat16),
            pltpu.SemaphoreType.DMA((11,)),
            pltpu.SemaphoreType.DMA((3,)),
        ],
        input_output_aliases=aliases,
        compiler_params=pltpu.CompilerParams(vmem_limit_bytes=GRANT),
        cost_estimate=pl.CostEstimate(
            flops=2 * total * 9 * inputs * outputs * RING,
            bytes_accessed=total * RING * (inputs + 3 * outputs) * 2,
            transcendentals=0,
        ),
        name="forward",
    )(*given)


def score_kernel(start, count, wraps, n_edges, adds, n_given, *refs):
    field, own_ref, other_ref, target_ref, weight_ref = refs[:3], *refs[3:7]
    edges = refs[7 : 7 + n_edges]
    sums_ref = refs[7 + n_edges] if adds else None
    turned_out, sums_out, slab_v, own_v, other_v, target_v, cot_v, acc_v, turned_v = refs[n_given:-2]
    in_sems, sems = refs[-2:]
    copies = start_all(
        [(own_ref, own_v), (other_ref, other_v)]
        + chunk_copies(slab_v, start, count, wraps, field, edges)
        + column_copies(target_ref, start, count, wraps, target_v),
        in_sems,
    )
    outputs, rows = target_ref.shape[1:]
    inputs = slab_v.shape[2]
    half = LANES // 2
    weight = weight_ref[...]
    cot_v[...] = jnp.zeros_like(cot_v)
    acc_v[...] = jnp.zeros_like(acc_v)
    clear_chunk(slab_v, count, wraps, rows)
    for copy in copies:
        copy.wait()

    def one(slot, column, place, block, odd, score):
        lanes_of_tail = slice(odd * half, odd * half + rows - LANES)
        halves = []
        for side in range(2):
            lanes = slice(0, LANES) if side == 0 else slice(LANES, rows)
            if side == 0:
                value, partner = (ref[slot].astype(jnp.float32) for ref in (own_v, other_v))
            else:
                value, partner = (
                    ref[block, :, lanes_of_tail].astype(jnp.float32) for ref in (own_v, other_v)
                )
            misfit = value - target_v[slot, :, lanes].astype(jnp.float32)
            spread = value - partner
            error2 = jnp.sum(misfit * misfit, axis=0, keepdims=True) + epsilon
            pair2 = jnp.sum(spread * spread, axis=0, keepdims=True) + epsilon
            error_inv = lax.rsqrt(error2)
            pair_inv = lax.rsqrt(pair2)
            scale = 0.5 * weight[:, lanes]
            cot_v[odd, :outputs, lanes] = misfit * (scale * error_inv) - spread * (scale * pair_inv)
            halves.append(scale * (error2 * error_inv - 0.5 * (pair2 * pair_inv)))
        cot = cot_v[odd]
        turned_v[slot] = cot.T[:rows].astype(jnp.bfloat16)
        if column is not None:
            write_pair(turned_v, turned_out, start, slot, odd, sems.at[0])
        cot = cot[:outputs]
        shifted = jnp.concatenate([pltpu.roll(cot, RING - 1, 1), cot, pltpu.roll(cot, 1, 1)], axis=0)
        acc_v[...] += jnp.dot(
            shifted.astype(jnp.bfloat16), window(slab_v, place), preferred_element_type=jnp.float32
        )
        return tuple(s + h for s, h in zip(score, halves))

    score = (jnp.zeros((1, LANES), jnp.float32), jnp.zeros((1, rows - LANES), jnp.float32))
    score = each_column(start, count, wraps, one, score)
    for a in range(3):
        for b in range(3):
            block = acc_v[a * outputs : (a + 1) * outputs, b * inputs : (b + 1) * inputs]
            place = slice((3 * a + b) * outputs, (3 * a + b + 1) * outputs)
            sums_out[place] = block + sums_ref[place] if adds else block
    spare = slice(9 * outputs, sums_out.shape[0])
    total = sum(jnp.sum(part, axis=1, keepdims=True) for part in score)
    filler = jnp.broadcast_to(total, (sums_out.shape[0] - 9 * outputs, inputs))
    sums_out[spare] = filler + sums_ref[spare] if adds else filler
    write_rest(turned_v, turned_out, start, count, wraps, sems)


def scored(start, count, wraps, field, own, other, target, weight, edges, carried, sum_rows):
    columns, outputs, rows = target.shape
    inputs = field[0].shape[2]
    total = count + wraps
    edges = list(edges) if wraps else []
    given = [*field, own, other, target, weight, *edges]
    in_specs = [HBM] * 6 + [VMEM] + [HBM] * len(edges)
    aliases = {}
    if carried is not None:
        turned, sums = carried
        aliases = {len(given) + 1: 0}
        given += [sums, turned]
        in_specs += [VMEM, HBM]
    return pl.pallas_call(
        functools.partial(
            score_kernel, start, count, wraps, len(edges), carried is not None, len(given)
        ),
        out_shape=(
            jax.ShapeDtypeStruct((columns, rows, LANES), jnp.bfloat16),
            jax.ShapeDtypeStruct((sum_rows, inputs), jnp.float32),
        ),
        in_specs=in_specs,
        out_specs=(HBM, VMEM),
        scratch_shapes=[
            pltpu.VMEM((count + 2 + 3 * wraps, RING, inputs), jnp.bfloat16),
            pltpu.VMEM(own.shape, jnp.bfloat16),
            pltpu.VMEM(own.shape, jnp.bfloat16),
            pltpu.VMEM((total, outputs, rows), jnp.bfloat16),
            pltpu.VMEM((2, LANES, RING), jnp.float32),
            pltpu.VMEM((3 * outputs, 3 * inputs), jnp.float32),
            pltpu.VMEM((total, rows, LANES), jnp.bfloat16),
            pltpu.SemaphoreType.DMA((12,)),
            pltpu.SemaphoreType.DMA((3,)),
        ],
        input_output_aliases=aliases,
        compiler_params=pltpu.CompilerParams(vmem_limit_bytes=GRANT),
        cost_estimate=pl.CostEstimate(
            flops=2 * total * 9 * inputs * outputs * RING,
            bytes_accessed=total * RING * (inputs + 3 * outputs) * 2,
            transcendentals=2 * total * rows,
        ),
        name="score",
    )(*given)


def backward_kernel(block, *refs):
    field, west_ref, east_ref, taps_ref, slope_out, slab_v, weights_v, sems = refs[:3], *refs[3:]
    rows, inputs = slope_out.shape[1:]
    columns = field[0].shape[0]
    outputs = taps_ref.shape[2]
    base = pl.program_id(0) * block

    @pl.when(pl.program_id(0) == 0)
    def _():
        copies = start_all(
            slab_copies(slab_v, 1, field, 0, columns)
            + [(west_ref, slab_v.at[pl.ds(0, 1)]), (east_ref, slab_v.at[pl.ds(columns + 1, 1)])],
            sems,
        )
        clear_gap(slab_v, slice(1, columns + 1), rows)
        spare = jnp.zeros((LANES - outputs, inputs), weights_v.dtype)
        for b in range(3):
            row = [jnp.concatenate([taps_ref[2 - a, 2 - b], spare], axis=0) for a in range(3)]
            weights_v[b * LANES : (b + 1) * LANES] = jnp.concatenate(row, axis=1)

        for copy in copies:
            copy.wait()

    for j in range(block):
        z = jnp.dot(window(slab_v, base + j), weights_v[...], preferred_element_type=jnp.float32)
        slope = (
            pltpu.roll(z[:, :inputs], 1, 0)
            + z[:, inputs : 2 * inputs]
            + pltpu.roll(z[:, 2 * inputs :], RING - 1, 0)
        )
        slope_out[j] = slope[:rows].astype(jnp.bfloat16)


def backward(field, edges, taps):
    columns, rows = field[0].shape[:2]
    inputs = taps.shape[3]
    block = max(n for n in range(1, 6) if columns % n == 0)
    return pl.pallas_call(
        functools.partial(backward_kernel, block),
        grid=(columns // block,),
        out_shape=jax.ShapeDtypeStruct((columns, rows, inputs), jnp.bfloat16),
        in_specs=[HBM] * 5 + [VMEM],
        out_specs=pl.BlockSpec((block, rows, inputs), lambda i: (i, 0, 0)),
        scratch_shapes=[
            pltpu.VMEM((columns + 2, RING, LANES), jnp.bfloat16),
            pltpu.VMEM((3 * LANES, 3 * inputs), jnp.bfloat16),
            pltpu.SemaphoreType.DMA((5,)),
        ],
        compiler_params=pltpu.CompilerParams(vmem_limit_bytes=GRANT),
        cost_estimate=pl.CostEstimate(
            flops=2 * columns * 9 * inputs * LANES * RING,
            bytes_accessed=columns * RING * (inputs + LANES) * 2,
            transcendentals=0,
        ),
        name="backward",
    )(*field, *edges, taps)


def exchange(blocks):
    return lax.all_to_all(blocks, AXES, 0, 0, tiled=True)


def split(columns):
    shares = (8, 14, 14, 9)
    edges = [1]
    for i in range(len(shares) - 1):
        edges.append(1 + 2 * round(columns * sum(shares[: i + 1]) / sum(shares) / 2))
    edges.append(columns)
    return [(low, high - low) for low, high in zip(edges, edges[1:])]


def local(features, present_condition, target, filter_weights_tensor):
    lat_rows, lon_cols, inputs = features.shape[1:]
    outputs = target.shape[2]
    total_rows = lat_rows * lax.axis_size("lat")
    total_cols = lon_cols * lax.axis_size("lon")
    devices = math.prod(lax.axis_size(axis) for axis in AXES)

    taps = jnp.transpose(filter_weights_tensor, (0, 1, 3, 2))
    row_index = lax.axis_index("lat") * lat_rows + jnp.arange(lat_rows, dtype=jnp.int32)
    weight = latitude_weights(row_index, total_rows)[None]
    columns = jnp.transpose(features[0], (1, 0, 2))
    present = jnp.transpose(present_condition[0], (1, 2, 0))
    truth = jnp.transpose(target, (1, 2, 0))

    field = (columns, *lat_edges(columns))
    edges = lon_edges(*field)
    chunks = split(lon_cols)
    pred = None
    packed = []
    for start, count in chunks:
        wraps = int(start + count == lon_cols)
        pred, own = forward(start, count, wraps, field, present, taps, edges, pred)
        packed.append((own, lax.ppermute(own, "member", [(0, 1), (1, 0)])))

    width = -(-(9 * outputs * inputs + 1) // (devices * LANES)) * LANES
    sum_rows = devices * width // inputs
    carried = None
    for (start, count), (own, other) in zip(chunks, packed):
        wraps = int(start + count == lon_cols)
        carried = scored(
            start, count, wraps, field, own, other, truth, weight, edges, carried, sum_rows
        )
    turned, sums = carried
    parts = exchange(sums.reshape(devices, width))
    field = (turned, *lat_edges(turned))
    share = jnp.sum(parts, axis=0, keepdims=True)
    share, edges = lax.optimization_barrier((share, lon_edges(*field)))
    whole = exchange(jnp.broadcast_to(share, (devices, width))).reshape(sum_rows, inputs)
    slope = backward(field, edges, taps)
    objective_mean = whole[9 * outputs, 0] / (total_rows * total_cols)
    summed = whole[: 9 * outputs] / math.sqrt(2.0 * total_rows * total_cols)
    filter_weights_slope = jnp.transpose(summed.reshape(3, 3, outputs, inputs), (0, 1, 3, 2))
    return (
        jnp.transpose(pred, (2, 0, 1))[None],
        objective_mean,
        jnp.transpose(slope, (1, 0, 2))[None],
        filter_weights_slope,
    )


def solution(mesh):
    in_specs = (
        P("member", "lat", "lon", None),
        P("member", "lat", "lon", None),
        P("lat", "lon", None),
        P(),
    )
    out_specs = (P("member", "lat", "lon", None), P(), P("member", "lat", "lon", None), P())
    return jax.shard_map(local, mesh=mesh, in_specs=in_specs, out_specs=out_specs, check_vma=False)
```

```python
import functools
import math

import jax
import jax.numpy as jnp
from jax import lax
from jax.experimental import pallas as pl
from jax.experimental.pallas import tpu as pltpu
from jax.sharding import PartitionSpec as P

epsilon = 1e-06
RING = 256
LANES = 128
TILE = 16
AXES = ("member", "lat", "lon")
VMEM = pl.BlockSpec(memory_space=pltpu.VMEM)
ANY = pl.BlockSpec(memory_space=pl.ANY)


def latitude_weights(row_index, total_rows):
    scale = math.pi / total_rows
    angles = 0.5 * math.pi - (row_index.astype(jnp.float32) + 0.5) * scale
    every_row = (
        0.5 * math.pi - (jnp.arange(total_rows, dtype=jnp.int32).astype(jnp.float32) + 0.5) * scale
    )
    return jnp.cos(angles) / jnp.mean(jnp.cos(every_row))


def swapped(first, last, axis, wraps):
    count = lax.axis_size(axis)
    even = lax.axis_index(axis) % 2 == 0
    inner = [(i, i + 1) for i in range(0, count, 2)]
    outer = [(i, (i + 1) % count) for i in range(1, count, 2) if wraps or i + 1 < count]
    both = [pairs + [(j, i) for i, j in pairs] for pairs in (inner, outer)]
    near = lax.ppermute(jnp.where(even, last, first), axis, both[0])
    far = lax.ppermute(jnp.where(even, first, last), axis, both[1])
    return jnp.where(even, far, near), jnp.where(even, near, far)


def lat_edges(columns):
    count, rows, channels = columns.shape
    body = rows - rows % TILE
    above, below = swapped(columns[:, :1], columns[:, rows - 1 :], "lat", False)
    gap = jnp.zeros((count, TILE - 1, channels), columns.dtype)
    low = jnp.concatenate([columns[:, body:], below, gap[:, : TILE - 1 - (rows - body)]], axis=1)
    return low, jnp.concatenate([gap, above], axis=1)


def lon_edges(columns, low, high):
    body = columns.shape[1] - columns.shape[1] % TILE

    def ring(part):
        gap = jnp.zeros((1, RING - body - 2 * TILE, columns.shape[2]), columns.dtype)
        return jnp.concatenate([columns[part, :body], low[part], gap, high[part]], axis=1)

    return swapped(ring(slice(0, 1)), ring(slice(-1, None)), "lon", True)


def ring_column(field, edges, column):
    field_ref, low_ref, high_ref = field
    if isinstance(column, int) and not 0 <= column < field_ref.shape[0]:
        return edges[0 if column < 0 else 1][0]
    body = field_ref.shape[1] - field_ref.shape[1] % TILE
    gap = jnp.zeros((RING - body - 2 * TILE, field_ref.shape[2]), field_ref.dtype)
    return jnp.concatenate([field_ref[column, :body], low_ref[column], gap, high_ref[column]], axis=0)


def window(field, edges, column):
    return jnp.concatenate([ring_column(field, edges, column + b - 1) for b in range(3)], axis=1)


def each_column(start, count, wraps, one, source_v, out, sems):
    total = count + wraps
    pairs = (count - wraps) // 2

    def pair(t, carry):
        one(2 * t, start + 2 * t, total + t, 0)
        one(2 * t + 1, start + 2 * t + 1, total + t, 1)
        to = out.at[pl.ds(start + 2 * t, 2)]
        pltpu.make_async_copy(source_v.at[pl.ds(2 * t, 2)], to, sems.at[0]).start()
        return carry

    lax.fori_loop(0, pairs, pair, 0)
    copies = []
    if pairs:
        span = pl.ds(0, 2 * pairs), pl.ds(start, 2 * pairs)
        copies.append(pltpu.make_async_copy(source_v.at[span[0]], out.at[span[1]], sems.at[0]))
    for slot in range(2 * pairs, total):
        column = start + slot if slot < count else 0
        one(slot, column, total + slot // 2, slot % 2)
        copy = pltpu.make_async_copy(
            source_v.at[pl.ds(slot, 1)], out.at[pl.ds(column, 1)], sems.at[1 + slot - 2 * pairs]
        )
        copy.start()
        copies.append(copy)
    for copy in copies:
        copy.wait()


def forward_kernel(start, count, wraps, n_given, *refs):
    field, present_ref, taps_ref = refs[:3], refs[3], refs[4]
    edges = refs[5:7] if wraps else ()
    pred_out, packed_out, weights_v, pred_v, sems = refs[n_given:]
    outputs, rows = present_ref.shape[1:]
    for a in range(3):
        weights_v[a * outputs : (a + 1) * outputs] = jnp.concatenate(
            [taps_ref[a, b] for b in range(3)], axis=1
        )
    half = LANES // 2

    def one(slot, column, block, odd):
        y = lax.dot_general(
            weights_v[...],
            window(field, edges, column),
            (((1,), (1,)), ((), ())),
            preferred_element_type=jnp.float32,
        )
        increment = (
            pltpu.roll(y[:outputs], 1, 1)
            + y[outputs : 2 * outputs]
            + pltpu.roll(y[2 * outputs :], RING - 1, 1)
        )
        head = increment[:, :LANES] + present_ref[column, :, :LANES].astype(jnp.float32)
        tail = increment[:, LANES:rows] + present_ref[column, :, LANES:].astype(jnp.float32)
        head = head.astype(jnp.bfloat16)
        tail = tail.astype(jnp.bfloat16)
        pred_v[slot, :, :LANES] = head
        pred_v[slot, :, LANES:] = tail
        packed_out[slot] = head
        packed_out[block, :, odd * half : odd * half + rows - LANES] = tail

    each_column(start, count, wraps, one, pred_v, pred_out, sems)


def forward(start, count, wraps, field, present, taps, edges, pred):
    columns, outputs, rows = present.shape
    inputs = taps.shape[3]
    total = count + wraps
    given = [*field, present, taps] + (list(edges) if wraps else [])
    in_specs = [VMEM] * len(given)
    aliases = {}
    if pred is not None:
        aliases = {len(given): 0}
        given.append(pred)
        in_specs.append(ANY)
    return pl.pallas_call(
        functools.partial(forward_kernel, start, count, wraps, len(given)),
        out_shape=(
            jax.ShapeDtypeStruct((columns, outputs, rows), jnp.bfloat16),
            jax.ShapeDtypeStruct((total + (total + 1) // 2, outputs, LANES), jnp.bfloat16),
        ),
        in_specs=in_specs,
        out_specs=(ANY, VMEM),
        scratch_shapes=[
            pltpu.VMEM((3 * outputs, 3 * inputs), jnp.bfloat16),
            pltpu.VMEM((total, outputs, rows), jnp.bfloat16),
            pltpu.SemaphoreType.DMA((4,)),
        ],
        input_output_aliases=aliases,
        compiler_params=pltpu.CompilerParams(vmem_limit_bytes=24 << 20),
        cost_estimate=pl.CostEstimate(
            flops=2 * total * 9 * inputs * outputs * RING,
            bytes_accessed=total * RING * (inputs + 3 * outputs) * 2,
            transcendentals=0,
        ),
        name="forward",
    )(*given)


def score_kernel(start, count, wraps, n_edges, adds, n_given, *refs):
    field, own_ref, other_ref, target_ref, weight_ref = refs[:3], *refs[3:7]
    edges = refs[7 : 7 + n_edges]
    sums_ref = refs[7 + n_edges] if adds else None
    turned_out, sums_out, cot_v, acc_v, score_v, turned_v, sems = refs[n_given:]
    outputs, rows = target_ref.shape[1:]
    inputs = field[0].shape[2]
    half = LANES // 2
    weight = weight_ref[...]
    cot_v[...] = jnp.zeros_like(cot_v)
    acc_v[...] = jnp.zeros_like(acc_v)
    score_v[...] = jnp.zeros_like(score_v)

    def one(slot, column, block, odd):
        lanes_of_tail = slice(odd * half, odd * half + rows - LANES)
        for side in range(2):
            lanes = slice(0, LANES) if side == 0 else slice(LANES, rows)
            if side == 0:
                value, partner = (ref[slot].astype(jnp.float32) for ref in (own_ref, other_ref))
            else:
                value, partner = (
                    ref[block, :, lanes_of_tail].astype(jnp.float32) for ref in (own_ref, other_ref)
                )
            misfit = value - target_ref[column, :, lanes].astype(jnp.float32)
            spread = value - partner
            error2 = jnp.sum(misfit * misfit, axis=0, keepdims=True) + epsilon
            pair2 = jnp.sum(spread * spread, axis=0, keepdims=True) + epsilon
            error_inv = lax.rsqrt(error2)
            pair_inv = lax.rsqrt(pair2)
            scale = 0.5 * weight[:, lanes]
            cot_v[odd, :outputs, lanes] = misfit * (scale * error_inv) - spread * (scale * pair_inv)
            score_v[:, lanes] += scale * (error2 * error_inv - 0.5 * (pair2 * pair_inv))
        cot = cot_v[odd]
        turned_v[slot] = cot.T[:rows].astype(jnp.bfloat16)
        cot = cot[:outputs]
        shifted = jnp.concatenate([pltpu.roll(cot, RING - 1, 1), cot, pltpu.roll(cot, 1, 1)], axis=0)
        acc_v[...] += jnp.dot(
            shifted.astype(jnp.bfloat16), window(field, edges, column), preferred_element_type=jnp.float32
        )

    each_column(start, count, wraps, one, turned_v, turned_out, sems)
    for a in range(3):
        for b in range(3):
            block = acc_v[a * outputs : (a + 1) * outputs, b * inputs : (b + 1) * inputs]
            place = slice((3 * a + b) * outputs, (3 * a + b + 1) * outputs)
            sums_out[place] = block + sums_ref[place] if adds else block
    spare = slice(9 * outputs, sums_out.shape[0])
    total = jnp.sum(score_v[...], axis=1, keepdims=True)
    filler = jnp.broadcast_to(total, (sums_out.shape[0] - 9 * outputs, inputs))
    sums_out[spare] = filler + sums_ref[spare] if adds else filler


def scored(start, count, wraps, field, own, other, target, weight, edges, carried, sum_rows):
    columns, outputs, rows = target.shape
    inputs = field[0].shape[2]
    total = count + wraps
    edges = list(edges) if wraps else []
    given = [*field, own, other, target, weight, *edges]
    in_specs = [VMEM] * len(given)
    aliases = {}
    if carried is not None:
        turned, sums = carried
        aliases = {len(given) + 1: 0}
        given += [sums, turned]
        in_specs += [VMEM, ANY]
    return pl.pallas_call(
        functools.partial(
            score_kernel, start, count, wraps, len(edges), carried is not None, len(given)
        ),
        out_shape=(
            jax.ShapeDtypeStruct((columns, rows, LANES), jnp.bfloat16),
            jax.ShapeDtypeStruct((sum_rows, inputs), jnp.float32),
        ),
        in_specs=in_specs,
        out_specs=(ANY, VMEM),
        scratch_shapes=[
            pltpu.VMEM((2, LANES, RING), jnp.float32),
            pltpu.VMEM((3 * outputs, 3 * inputs), jnp.float32),
            pltpu.VMEM((1, RING), jnp.float32),
            pltpu.VMEM((total, rows, LANES), jnp.bfloat16),
            pltpu.SemaphoreType.DMA((4,)),
        ],
        input_output_aliases=aliases,
        compiler_params=pltpu.CompilerParams(vmem_limit_bytes=24 << 20),
        cost_estimate=pl.CostEstimate(
            flops=2 * total * 9 * inputs * outputs * RING,
            bytes_accessed=total * RING * (inputs + 3 * outputs) * 2,
            transcendentals=2 * total * rows,
        ),
        name="score",
    )(*given)


def backward_kernel(block, *refs):
    field, west_ref, east_ref, taps_ref, slope_out, weights_v = refs[:3], *refs[3:]
    rows, inputs = slope_out.shape[1:]
    columns = field[0].shape[0]
    outputs = taps_ref.shape[2]
    base = pl.program_id(0) * block

    @pl.when(pl.program_id(0) == 0)
    def _():
        spare = jnp.zeros((LANES - outputs, inputs), weights_v.dtype)
        for b in range(3):
            row = [jnp.concatenate([taps_ref[2 - a, 2 - b], spare], axis=0) for a in range(3)]
            weights_v[b * LANES : (b + 1) * LANES] = jnp.concatenate(row, axis=1)

    def halo_column(j):
        at = base + j
        inner = ring_column(field, (), jnp.clip(at, 0, columns - 1))
        if j == -1:
            return jnp.where(at < 0, west_ref[0], inner)
        return jnp.where(at == columns, east_ref[0], inner) if j == block else inner

    ring = [halo_column(j) for j in range(-1, block + 1)]
    for j in range(block):
        z = jnp.dot(
            jnp.concatenate(ring[j : j + 3], axis=1),
            weights_v[...],
            preferred_element_type=jnp.float32,
        )
        slope = (
            pltpu.roll(z[:, :inputs], 1, 0)
            + z[:, inputs : 2 * inputs]
            + pltpu.roll(z[:, 2 * inputs :], RING - 1, 0)
        )
        slope_out[j] = slope[:rows].astype(jnp.bfloat16)


def backward(field, edges, taps):
    columns, rows = field[0].shape[:2]
    inputs = taps.shape[3]
    block = max(n for n in range(1, 6) if columns % n == 0)
    return pl.pallas_call(
        functools.partial(backward_kernel, block),
        grid=(columns // block,),
        out_shape=jax.ShapeDtypeStruct((columns, rows, inputs), jnp.bfloat16),
        in_specs=[VMEM] * 6,
        out_specs=pl.BlockSpec((block, rows, inputs), lambda i: (i, 0, 0)),
        scratch_shapes=[
            pltpu.VMEM((3 * LANES, 3 * inputs), jnp.bfloat16),
        ],
        compiler_params=pltpu.CompilerParams(vmem_limit_bytes=24 << 20),
        cost_estimate=pl.CostEstimate(
            flops=2 * columns * 9 * inputs * LANES * RING,
            bytes_accessed=columns * RING * (inputs + LANES) * 2,
            transcendentals=0,
        ),
        name="backward",
    )(*field, *edges, taps)


def exchange(blocks):
    return lax.all_to_all(blocks, AXES, 0, 0, tiled=True)


def split(columns):
    shares = (8, 14, 14, 9)
    edges = [1]
    for i in range(len(shares) - 1):
        edges.append(1 + 2 * round(columns * sum(shares[: i + 1]) / sum(shares) / 2))
    edges.append(columns)
    return [(low, high - low) for low, high in zip(edges, edges[1:])]


def local(features, present_condition, target, filter_weights_tensor):
    lat_rows, lon_cols, inputs = features.shape[1:]
    outputs = target.shape[2]
    total_rows = lat_rows * lax.axis_size("lat")
    total_cols = lon_cols * lax.axis_size("lon")
    devices = math.prod(lax.axis_size(axis) for axis in AXES)

    taps = jnp.transpose(filter_weights_tensor, (0, 1, 3, 2))
    row_index = lax.axis_index("lat") * lat_rows + jnp.arange(lat_rows, dtype=jnp.int32)
    weight = latitude_weights(row_index, total_rows)[None]
    columns = jnp.transpose(features[0], (1, 0, 2))
    present = jnp.transpose(present_condition[0], (1, 2, 0))
    truth = jnp.transpose(target, (1, 2, 0))

    field = (columns, *lat_edges(columns))
    edges = lon_edges(*field)
    chunks = split(lon_cols)
    pred = None
    packed = []
    for start, count in chunks:
        wraps = int(start + count == lon_cols)
        pred, own = forward(start, count, wraps, field, present, taps, edges, pred)
        packed.append((own, lax.ppermute(own, "member", [(0, 1), (1, 0)])))

    width = -(-(9 * outputs * inputs + 1) // (devices * LANES)) * LANES
    sum_rows = devices * width // inputs
    carried = None
    for (start, count), (own, other) in zip(chunks, packed):
        wraps = int(start + count == lon_cols)
        carried = scored(
            start, count, wraps, field, own, other, truth, weight, edges, carried, sum_rows
        )
    turned, sums = carried
    share = jnp.sum(exchange(sums.reshape(devices, width)), axis=0, keepdims=True)
    field = (turned, *lat_edges(turned))
    share, edges = lax.optimization_barrier((share, lon_edges(*field)))
    whole = exchange(jnp.broadcast_to(share, (devices, width))).reshape(sum_rows, inputs)
    slope = backward(field, edges, taps)
    objective_mean = whole[9 * outputs, 0] / (total_rows * total_cols)
    summed = whole[: 9 * outputs] / math.sqrt(2.0 * total_rows * total_cols)
    filter_weights_slope = jnp.transpose(summed.reshape(3, 3, outputs, inputs), (0, 1, 3, 2))
    return (
        jnp.transpose(pred, (2, 0, 1))[None],
        objective_mean,
        jnp.transpose(slope, (1, 0, 2))[None],
        filter_weights_slope,
    )


def solution(mesh):
    in_specs = (
        P("member", "lat", "lon", None),
        P("member", "lat", "lon", None),
        P("lat", "lon", None),
        P(),
    )
    out_specs = (P("member", "lat", "lon", None), P(), P("member", "lat", "lon", None), P())
    return jax.shard_map(local, mesh=mesh, in_specs=in_specs, out_specs=out_specs, check_vma=False)
```

```python
import functools
import math

import jax
import jax.numpy as jnp
from jax import lax
from jax.experimental import pallas as pl
from jax.experimental.pallas import tpu as pltpu
from jax.sharding import PartitionSpec as P

epsilon = 1e-06
RING = 256
LANES = 128
TILE = 16
AXES = ("member", "lat", "lon")
VMEM = pl.BlockSpec(memory_space=pltpu.VMEM)
ANY = pl.BlockSpec(memory_space=pl.ANY)


def latitude_weights(row_index, total_rows):
    scale = math.pi / total_rows
    angles = 0.5 * math.pi - (row_index.astype(jnp.float32) + 0.5) * scale
    mean = sum(math.cos(0.5 * math.pi - (r + 0.5) * scale) for r in range(total_rows)) / total_rows
    return jnp.cos(angles) * (1.0 / mean)


def swapped(first, last, axis, wraps):
    count = lax.axis_size(axis)
    even = lax.axis_index(axis) % 2 == 0
    inner = [(i, i + 1) for i in range(0, count, 2)]
    outer = [(i, (i + 1) % count) for i in range(1, count, 2) if wraps or i + 1 < count]
    both = [pairs + [(j, i) for i, j in pairs] for pairs in (inner, outer)]
    near = lax.ppermute(jnp.where(even, last, first), axis, both[0])
    far = lax.ppermute(jnp.where(even, first, last), axis, both[1])
    return jnp.where(even, far, near), jnp.where(even, near, far)


def lat_edges(columns):
    count, rows, channels = columns.shape
    body = rows - rows % TILE
    above, below = swapped(columns[:, :1], columns[:, rows - 1 :], "lat", False)
    gap = jnp.zeros((count, TILE - 1, channels), columns.dtype)
    low = jnp.concatenate([columns[:, body:], below, gap[:, : TILE - 1 - (rows - body)]], axis=1)
    return low, jnp.concatenate([gap, above], axis=1)


def lon_edges(columns, low, high):
    body = columns.shape[1] - columns.shape[1] % TILE

    def ring(part):
        gap = jnp.zeros((1, RING - body - 2 * TILE, columns.shape[2]), columns.dtype)
        return jnp.concatenate([columns[part, :body], low[part], gap, high[part]], axis=1)

    return swapped(ring(slice(0, 1)), ring(slice(-1, None)), "lon", True)


def ring_column(field, edges, column):
    field_ref, low_ref, high_ref = field
    if isinstance(column, int) and not 0 <= column < field_ref.shape[0]:
        return edges[0 if column < 0 else 1][0]
    body = field_ref.shape[1] - field_ref.shape[1] % TILE
    gap = jnp.zeros((RING - body - 2 * TILE, field_ref.shape[2]), field_ref.dtype)
    return jnp.concatenate([field_ref[column, :body], low_ref[column], gap, high_ref[column]], axis=0)


def window(field, edges, column):
    return jnp.concatenate([ring_column(field, edges, column + b - 1) for b in range(3)], axis=1)


def each_pair(start, count, wraps, two, source_v, out, sems):
    total = count + wraps
    pairs = (count - wraps) // 2

    def pair(t, carry):
        two(2 * t, (start + 2 * t, start + 2 * t + 1))
        to = out.at[pl.ds(start + 2 * t, 2)]
        pltpu.make_async_copy(source_v.at[pl.ds(2 * t, 2)], to, sems.at[0]).start()
        return carry

    lax.fori_loop(0, pairs, pair, 0)
    copies = []
    if pairs:
        span = pl.ds(0, 2 * pairs), pl.ds(start, 2 * pairs)
        copies.append(pltpu.make_async_copy(source_v.at[span[0]], out.at[span[1]], sems.at[0]))
    columns = [start + slot if slot < count else 0 for slot in range(total)]
    for slot in range(2 * pairs, total, 2):
        two(slot, tuple(columns[slot : slot + 2]))
        for i in range(slot, min(slot + 2, total)):
            copy = pltpu.make_async_copy(
                source_v.at[pl.ds(i, 1)], out.at[pl.ds(columns[i], 1)], sems.at[1 + i - 2 * pairs]
            )
            copy.start()
            copies.append(copy)
    for copy in copies:
        copy.wait()


def together(low, high):
    lane = lax.broadcasted_iota(jnp.int32, low.shape, 1)
    return jnp.where(lane < LANES // 2, low, pltpu.roll(high, LANES // 2, 1))


def forward_kernel(start, count, wraps, n_given, *refs):
    field, present_ref, taps_ref = refs[:3], refs[3], refs[4]
    edges = refs[5:7] if wraps else ()
    pred_out, packed_out, weights_v, tails_v, pred_v, sems = refs[n_given:]
    outputs, rows = present_ref.shape[1:]
    for a in range(3):
        weights_v[a * outputs : (a + 1) * outputs] = jnp.concatenate(
            [taps_ref[a, b] for b in range(3)], axis=1
        )
    total = count + wraps
    tails_v[...] = jnp.zeros_like(tails_v)

    def one(slot, column, odd):
        y = lax.dot_general(
            weights_v[...],
            window(field, edges, column),
            (((1,), (1,)), ((), ())),
            preferred_element_type=jnp.float32,
        )
        increment = (
            pltpu.roll(y[:outputs], 1, 1)
            + y[outputs : 2 * outputs]
            + pltpu.roll(y[2 * outputs :], RING - 1, 1)
        )
        head = increment[:, :LANES] + present_ref[column, :, :LANES].astype(jnp.float32)
        tail = increment[:, LANES:rows] + present_ref[column, :, LANES:].astype(jnp.float32)
        head = head.astype(jnp.bfloat16)
        tail = tail.astype(jnp.bfloat16)
        pred_v[slot, :, :LANES] = head
        pred_v[slot, :, LANES:] = tail
        packed_out[slot] = head
        tails_v[odd, :, : rows - LANES] = tail.astype(jnp.float32)

    def two(slot, columns):
        for i, column in enumerate(columns):
            one(slot + i, column, i)
        packed_out[total + slot // 2] = together(tails_v[0], tails_v[1]).astype(jnp.bfloat16)

    each_pair(start, count, wraps, two, pred_v, pred_out, sems)


def forward(start, count, wraps, field, present, taps, edges, pred):
    columns, outputs, rows = present.shape
    inputs = taps.shape[3]
    total = count + wraps
    given = [*field, present, taps] + (list(edges) if wraps else [])
    in_specs = [VMEM] * len(given)
    aliases = {}
    if pred is not None:
        aliases = {len(given): 0}
        given.append(pred)
        in_specs.append(ANY)
    return pl.pallas_call(
        functools.partial(forward_kernel, start, count, wraps, len(given)),
        out_shape=(
            jax.ShapeDtypeStruct((columns, outputs, rows), jnp.bfloat16),
            jax.ShapeDtypeStruct((total + (total + 1) // 2, outputs, LANES), jnp.bfloat16),
        ),
        in_specs=in_specs,
        out_specs=(ANY, VMEM),
        scratch_shapes=[
            pltpu.VMEM((3 * outputs, 3 * inputs), jnp.bfloat16),
            pltpu.VMEM((2, outputs, LANES), jnp.float32),
            pltpu.VMEM((total, outputs, rows), jnp.bfloat16),
            pltpu.SemaphoreType.DMA((4,)),
        ],
        input_output_aliases=aliases,
        compiler_params=pltpu.CompilerParams(vmem_limit_bytes=24 << 20),
        cost_estimate=pl.CostEstimate(
            flops=2 * total * 9 * inputs * outputs * RING,
            bytes_accessed=total * RING * (inputs + 3 * outputs) * 2,
            transcendentals=0,
        ),
        name="forward",
    )(*given)


def score_kernel(start, count, wraps, n_edges, adds, n_given, *refs):
    field, own_ref, other_ref, target_ref, weight_ref = refs[:3], *refs[3:7]
    edges = refs[7 : 7 + n_edges]
    sums_ref = refs[7 + n_edges] if adds else None
    turned_out, sums_out, cot_v, acc_v, score_v, tails_v, turned_v, sems = refs[n_given:]
    outputs, rows = target_ref.shape[1:]
    inputs = field[0].shape[2]
    total = count + wraps
    tail = rows - LANES
    half_weight = 0.5 * weight_ref[...]
    cot_v[...] = jnp.zeros_like(cot_v)
    acc_v[...] = jnp.zeros_like(acc_v)
    score_v[...] = jnp.zeros_like(score_v)
    tails_v[...] = jnp.zeros_like(tails_v)

    def gradient(value, partner, truth, scale, lanes):
        misfit = value - truth
        spread = value - partner
        error2 = jnp.sum(misfit * misfit, axis=0, keepdims=True) + epsilon
        pair2 = jnp.sum(spread * spread, axis=0, keepdims=True) + epsilon
        error_inv = lax.rsqrt(error2)
        pair_inv = lax.rsqrt(pair2)
        score_v[:, lanes] += scale * (error2 * error_inv - 0.5 * (pair2 * pair_inv))
        return misfit * (scale * error_inv) - spread * (scale * pair_inv)

    def two(slot, columns):
        for i, column in enumerate(columns):
            cot_v[i, :outputs, :LANES] = gradient(
                own_ref[slot + i].astype(jnp.float32),
                other_ref[slot + i].astype(jnp.float32),
                target_ref[column, :, :LANES].astype(jnp.float32),
                half_weight[:, :LANES],
                slice(0, LANES),
            )
            tails_v[i, :, :tail] = target_ref[column, :, LANES:].astype(jnp.float32)
        block = total + slot // 2
        ends = gradient(
            own_ref[block].astype(jnp.float32),
            other_ref[block].astype(jnp.float32),
            together(tails_v[0], tails_v[1]),
            half_weight[:, LANES:] if len(columns) == 2 else single_weight,
            slice(LANES, 2 * LANES),
        )
        cot_v[0, :outputs, LANES:rows] = ends[:, :tail]
        if len(columns) == 2:
            cot_v[1, :outputs, LANES:rows] = pltpu.roll(ends, LANES // 2, 1)[:, :tail]
        for i, column in enumerate(columns):
            cot = cot_v[i]
            turned_v[slot + i] = cot.T[:rows].astype(jnp.bfloat16)
            cot = cot[:outputs]
            shifted = jnp.concatenate(
                [pltpu.roll(cot, RING - 1, 1), cot, pltpu.roll(cot, 1, 1)], axis=0
            )
            acc_v[...] += jnp.dot(
                shifted.astype(jnp.bfloat16),
                window(field, edges, column),
                preferred_element_type=jnp.float32,
            )

    lane = lax.broadcasted_iota(jnp.int32, (1, LANES), 1)
    single_weight = jnp.where(lane < LANES // 2, half_weight[:, LANES:], 0.0)
    each_pair(start, count, wraps, two, turned_v, turned_out, sems)
    for a in range(3):
        for b in range(3):
            block = acc_v[a * outputs : (a + 1) * outputs, b * inputs : (b + 1) * inputs]
            place = slice((3 * a + b) * outputs, (3 * a + b + 1) * outputs)
            sums_out[place] = block + sums_ref[place] if adds else block
    spare = slice(9 * outputs, sums_out.shape[0])
    whole = jnp.sum(score_v[...], axis=1, keepdims=True)
    filler = jnp.broadcast_to(whole, (sums_out.shape[0] - 9 * outputs, inputs))
    sums_out[spare] = filler + sums_ref[spare] if adds else filler


def scored(start, count, wraps, field, own, other, target, weight, edges, carried, sum_rows):
    columns, outputs, rows = target.shape
    inputs = field[0].shape[2]
    total = count + wraps
    edges = list(edges) if wraps else []
    given = [*field, own, other, target, weight, *edges]
    in_specs = [VMEM] * len(given)
    aliases = {}
    if carried is not None:
        turned, sums = carried
        aliases = {len(given) + 1: 0}
        given += [sums, turned]
        in_specs += [VMEM, ANY]
    return pl.pallas_call(
        functools.partial(
            score_kernel, start, count, wraps, len(edges), carried is not None, len(given)
        ),
        out_shape=(
            jax.ShapeDtypeStruct((columns, rows, LANES), jnp.bfloat16),
            jax.ShapeDtypeStruct((sum_rows, inputs), jnp.float32),
        ),
        in_specs=in_specs,
        out_specs=(ANY, VMEM),
        scratch_shapes=[
            pltpu.VMEM((2, LANES, RING), jnp.float32),
            pltpu.VMEM((3 * outputs, 3 * inputs), jnp.float32),
            pltpu.VMEM((1, 2 * LANES), jnp.float32),
            pltpu.VMEM((2, outputs, LANES), jnp.float32),
            pltpu.VMEM((total, rows, LANES), jnp.bfloat16),
            pltpu.SemaphoreType.DMA((4,)),
        ],
        input_output_aliases=aliases,
        compiler_params=pltpu.CompilerParams(vmem_limit_bytes=24 << 20),
        cost_estimate=pl.CostEstimate(
            flops=2 * total * 9 * inputs * outputs * RING,
            bytes_accessed=total * RING * (inputs + 3 * outputs) * 2,
            transcendentals=2 * total * rows,
        ),
        name="score",
    )(*given)


def backward_kernel(block, *refs):
    field, west_ref, east_ref, taps_ref, slope_out, weights_v = refs[:3], *refs[3:]
    rows, inputs = slope_out.shape[1:]
    columns = field[0].shape[0]
    outputs = taps_ref.shape[2]
    base = pl.program_id(0) * block

    @pl.when(pl.program_id(0) == 0)
    def _():
        spare = jnp.zeros((LANES - outputs, inputs), weights_v.dtype)
        for b in range(3):
            row = [jnp.concatenate([taps_ref[2 - a, 2 - b], spare], axis=0) for a in range(3)]
            weights_v[b * LANES : (b + 1) * LANES] = jnp.concatenate(row, axis=1)

    def halo_column(j):
        at = base + j
        inner = ring_column(field, (), jnp.clip(at, 0, columns - 1))
        if j == -1:
            return jnp.where(at < 0, west_ref[0], inner)
        return jnp.where(at == columns, east_ref[0], inner) if j == block else inner

    ring = [halo_column(j) for j in range(-1, block + 1)]
    for j in range(block):
        z = jnp.dot(
            jnp.concatenate(ring[j : j + 3], axis=1),
            weights_v[...],
            preferred_element_type=jnp.float32,
        )
        slope = (
            pltpu.roll(z[:, :inputs], 1, 0)
            + z[:, inputs : 2 * inputs]
            + pltpu.roll(z[:, 2 * inputs :], RING - 1, 0)
        )
        slope_out[j] = slope[:rows].astype(jnp.bfloat16)


def backward(field, edges, taps):
    columns, rows = field[0].shape[:2]
    inputs = taps.shape[3]
    block = max(n for n in range(1, 6) if columns % n == 0)
    return pl.pallas_call(
        functools.partial(backward_kernel, block),
        grid=(columns // block,),
        out_shape=jax.ShapeDtypeStruct((columns, rows, inputs), jnp.bfloat16),
        in_specs=[VMEM] * 6,
        out_specs=pl.BlockSpec((block, rows, inputs), lambda i: (i, 0, 0)),
        scratch_shapes=[
            pltpu.VMEM((3 * LANES, 3 * inputs), jnp.bfloat16),
        ],
        compiler_params=pltpu.CompilerParams(vmem_limit_bytes=24 << 20),
        cost_estimate=pl.CostEstimate(
            flops=2 * columns * 9 * inputs * LANES * RING,
            bytes_accessed=columns * RING * (inputs + LANES) * 2,
            transcendentals=0,
        ),
        name="backward",
    )(*field, *edges, taps)


def exchange(blocks):
    return lax.all_to_all(blocks, AXES, 0, 0, tiled=True)


def split(columns):
    shares = (12, 18, 15)
    edges = [1]
    for i in range(len(shares) - 1):
        edges.append(1 + 2 * round(columns * sum(shares[: i + 1]) / sum(shares) / 2))
    edges.append(columns)
    return [(low, high - low) for low, high in zip(edges, edges[1:])]


def local(features, present_condition, target, filter_weights_tensor):
    lat_rows, lon_cols, inputs = features.shape[1:]
    outputs = target.shape[2]
    total_rows = lat_rows * lax.axis_size("lat")
    total_cols = lon_cols * lax.axis_size("lon")
    devices = math.prod(lax.axis_size(axis) for axis in AXES)

    taps = jnp.transpose(filter_weights_tensor, (0, 1, 3, 2))
    row_index = lax.axis_index("lat") * lat_rows + jnp.arange(lat_rows, dtype=jnp.int32)
    weight = latitude_weights(row_index, total_rows)
    ends = jnp.pad(weight[LANES:], (0, LANES + LANES // 2 - lat_rows))
    weight = jnp.concatenate([weight[:LANES], ends, ends])[None]
    columns = jnp.transpose(features[0], (1, 0, 2))
    present = jnp.transpose(present_condition[0], (1, 2, 0))
    truth = jnp.transpose(target, (1, 2, 0))

    field = (columns, *lat_edges(columns))
    edges = lon_edges(*field)
    chunks = split(lon_cols)
    pred = None
    packed = []
    for start, count in chunks:
        wraps = int(start + count == lon_cols)
        pred, own = forward(start, count, wraps, field, present, taps, edges, pred)
        packed.append((own, lax.ppermute(own, "member", [(0, 1), (1, 0)])))

    width = -(-(9 * outputs * inputs + 1) // (devices * LANES)) * LANES
    sum_rows = devices * width // inputs
    carried = None
    for (start, count), (own, other) in zip(chunks, packed):
        wraps = int(start + count == lon_cols)
        carried = scored(
            start, count, wraps, field, own, other, truth, weight, edges, carried, sum_rows
        )
    turned, sums = carried
    share = jnp.sum(exchange(sums.reshape(devices, width)), axis=0, keepdims=True)
    field = (turned, *lat_edges(turned))
    share, edges = lax.optimization_barrier((share, lon_edges(*field)))
    whole = exchange(jnp.broadcast_to(share, (devices, width))).reshape(sum_rows, inputs)
    slope = backward(field, edges, taps)
    objective_mean = whole[9 * outputs, 0] / (total_rows * total_cols)
    summed = whole[: 9 * outputs] / math.sqrt(2.0 * total_rows * total_cols)
    filter_weights_slope = jnp.transpose(summed.reshape(3, 3, outputs, inputs), (0, 1, 3, 2))
    return (
        jnp.transpose(pred, (2, 0, 1))[None],
        objective_mean,
        jnp.transpose(slope, (1, 0, 2))[None],
        filter_weights_slope,
    )


def solution(mesh):
    in_specs = (
        P("member", "lat", "lon", None),
        P("member", "lat", "lon", None),
        P("lat", "lon", None),
        P(),
    )
    out_specs = (P("member", "lat", "lon", None), P(), P("member", "lat", "lon", None), P())
    return jax.shard_map(local, mesh=mesh, in_specs=in_specs, out_specs=out_specs, check_vma=False)
```

```python
import functools
import math

import jax
import jax.numpy as jnp
from jax import lax
from jax.experimental import pallas as pl
from jax.experimental.pallas import tpu as pltpu
from jax.sharding import PartitionSpec as P

epsilon = 1e-06
RING = 256
LANES = 128
TILE = 16
AXES = ("member", "lat", "lon")
VMEM = pl.BlockSpec(memory_space=pltpu.VMEM)
ANY = pl.BlockSpec(memory_space=pl.ANY)


def latitude_weights(row_index, total_rows):
    scale = math.pi / total_rows
    angles = 0.5 * math.pi - (row_index.astype(jnp.float32) + 0.5) * scale
    mean = sum(math.cos(0.5 * math.pi - (r + 0.5) * scale) for r in range(total_rows)) / total_rows
    return jnp.cos(angles) * (1.0 / mean)


def swapped(first, last, axis, wraps):
    count = lax.axis_size(axis)
    even = lax.axis_index(axis) % 2 == 0
    inner = [(i, i + 1) for i in range(0, count, 2)]
    outer = [(i, (i + 1) % count) for i in range(1, count, 2) if wraps or i + 1 < count]
    both = [pairs + [(j, i) for i, j in pairs] for pairs in (inner, outer)]
    near = lax.ppermute(jnp.where(even, last, first), axis, both[0])
    far = lax.ppermute(jnp.where(even, first, last), axis, both[1])
    return jnp.where(even, far, near), jnp.where(even, near, far)


def lat_edges(columns):
    count, rows, channels = columns.shape
    body = rows - rows % TILE
    above, below = swapped(columns[:, :1], columns[:, rows - 1 :], "lat", False)
    gap = jnp.zeros((count, TILE - 1, channels), columns.dtype)
    low = jnp.concatenate([columns[:, body:], below, gap[:, : TILE - 1 - (rows - body)]], axis=1)
    return low, jnp.concatenate([gap, above], axis=1)


def lon_rings(columns, low, high):
    body = columns.shape[1] - columns.shape[1] % TILE

    def ring(part):
        gap = jnp.zeros((1, RING - body - 2 * TILE, columns.shape[2]), columns.dtype)
        return jnp.concatenate([columns[part, :body], low[part], gap, high[part]], axis=1)

    return ring(slice(0, 1)), ring(slice(-1, None))


def lon_edges(rings):
    return swapped(*rings, "lon", True)


def ring_column(field, edges, column):
    field_ref, low_ref, high_ref = field
    if isinstance(column, int) and not 0 <= column < field_ref.shape[0]:
        return edges[0 if column < 0 else 1][0]
    body = field_ref.shape[1] - field_ref.shape[1] % TILE
    gap = jnp.zeros((RING - body - 2 * TILE, field_ref.shape[2]), field_ref.dtype)
    return jnp.concatenate([field_ref[column, :body], low_ref[column], gap, high_ref[column]], axis=0)


def window(field, edges, column):
    return jnp.concatenate([ring_column(field, edges, column + b - 1) for b in range(3)], axis=1)


def each_pair(start, count, wraps, two, source_v, out, sems):
    total = count + wraps
    pairs = (count - wraps) // 2

    def pair(t, carry):
        two(2 * t, (start + 2 * t, start + 2 * t + 1))
        to = out.at[pl.ds(start + 2 * t, 2)]
        pltpu.make_async_copy(source_v.at[pl.ds(2 * t, 2)], to, sems.at[0]).start()
        return carry

    lax.fori_loop(0, pairs, pair, 0)
    copies = []
    if pairs:
        span = pl.ds(0, 2 * pairs), pl.ds(start, 2 * pairs)
        copies.append(pltpu.make_async_copy(source_v.at[span[0]], out.at[span[1]], sems.at[0]))
    columns = [start + slot if slot < count else 0 for slot in range(total)]
    for slot in range(2 * pairs, total, 2):
        two(slot, tuple(columns[slot : slot + 2]))
        for i in range(slot, min(slot + 2, total)):
            copy = pltpu.make_async_copy(
                source_v.at[pl.ds(i, 1)], out.at[pl.ds(columns[i], 1)], sems.at[1 + i - 2 * pairs]
            )
            copy.start()
            copies.append(copy)
    for copy in copies:
        copy.wait()


def together(low, high):
    lane = lax.broadcasted_iota(jnp.int32, low.shape, 1)
    return jnp.where(lane < LANES // 2, low, pltpu.roll(high, LANES // 2, 1))


def forward_kernel(start, count, wraps, n_given, *refs):
    field, present_ref, taps_ref = refs[:3], refs[3], refs[4]
    edges = refs[5:7] if wraps else ()
    pred_out, packed_out, weights_v, tails_v, pred_v, sems = refs[n_given:]
    outputs, rows = present_ref.shape[1:]
    for a in range(3):
        weights_v[a * outputs : (a + 1) * outputs] = jnp.concatenate(
            [taps_ref[a, b] for b in range(3)], axis=1
        )
    total = count + wraps
    tails_v[...] = jnp.zeros_like(tails_v)

    def one(slot, column, odd):
        y = lax.dot_general(
            weights_v[...],
            window(field, edges, column),
            (((1,), (1,)), ((), ())),
            preferred_element_type=jnp.float32,
        )
        increment = (
            pltpu.roll(y[:outputs], 1, 1)
            + y[outputs : 2 * outputs]
            + pltpu.roll(y[2 * outputs :], RING - 1, 1)
        )
        head = increment[:, :LANES] + present_ref[column, :, :LANES].astype(jnp.float32)
        tail = increment[:, LANES:rows] + present_ref[column, :, LANES:].astype(jnp.float32)
        head = head.astype(jnp.bfloat16)
        tail = tail.astype(jnp.bfloat16)
        pred_v[slot, :, :LANES] = head
        pred_v[slot, :, LANES:] = tail
        packed_out[slot] = head
        tails_v[odd, :, : rows - LANES] = tail.astype(jnp.float32)

    def two(slot, columns):
        for i, column in enumerate(columns):
            one(slot + i, column, i)
        packed_out[total + slot // 2] = together(tails_v[0], tails_v[1]).astype(jnp.bfloat16)

    each_pair(start, count, wraps, two, pred_v, pred_out, sems)


def forward(start, count, wraps, field, present, taps, edges, pred):
    columns, outputs, rows = present.shape
    inputs = taps.shape[3]
    total = count + wraps
    given = [*field, present, taps] + (list(edges) if wraps else [])
    in_specs = [VMEM] * len(given)
    aliases = {}
    if pred is not None:
        aliases = {len(given): 0}
        given.append(pred)
        in_specs.append(ANY)
    return pl.pallas_call(
        functools.partial(forward_kernel, start, count, wraps, len(given)),
        out_shape=(
            jax.ShapeDtypeStruct((columns, outputs, rows), jnp.bfloat16),
            jax.ShapeDtypeStruct((total + (total + 1) // 2, outputs, LANES), jnp.bfloat16),
        ),
        in_specs=in_specs,
        out_specs=(ANY, VMEM),
        scratch_shapes=[
            pltpu.VMEM((3 * outputs, 3 * inputs), jnp.bfloat16),
            pltpu.VMEM((2, outputs, LANES), jnp.float32),
            pltpu.VMEM((total, outputs, rows), jnp.bfloat16),
            pltpu.SemaphoreType.DMA((4,)),
        ],
        input_output_aliases=aliases,
        compiler_params=pltpu.CompilerParams(vmem_limit_bytes=24 << 20),
        cost_estimate=pl.CostEstimate(
            flops=2 * total * 9 * inputs * outputs * RING,
            bytes_accessed=total * RING * (inputs + 3 * outputs) * 2,
            transcendentals=0,
        ),
        name="forward",
    )(*given)


def score_kernel(start, count, wraps, n_edges, adds, n_given, *refs):
    field, own_ref, other_ref, target_ref, weight_ref = refs[:3], *refs[3:7]
    edges = refs[7 : 7 + n_edges]
    sums_ref = refs[7 + n_edges] if adds else None
    turned_out, sums_out, cot_v, acc_v, score_v, tails_v, turned_v, sems = refs[n_given:]
    outputs, rows = target_ref.shape[1:]
    inputs = field[0].shape[2]
    total = count + wraps
    tail = rows - LANES
    half_weight = 0.5 * weight_ref[...]
    cot_v[...] = jnp.zeros_like(cot_v)
    acc_v[...] = jnp.zeros_like(acc_v)
    score_v[...] = jnp.zeros_like(score_v)
    tails_v[...] = jnp.zeros_like(tails_v)

    def gradient(value, partner, truth, scale, lanes):
        misfit = value - truth
        spread = value - partner
        error2 = jnp.sum(misfit * misfit, axis=0, keepdims=True) + epsilon
        pair2 = jnp.sum(spread * spread, axis=0, keepdims=True) + epsilon
        error_inv = lax.rsqrt(error2)
        pair_inv = lax.rsqrt(pair2)
        score_v[:, lanes] += scale * (error2 * error_inv - 0.5 * (pair2 * pair_inv))
        return misfit * (scale * error_inv) - spread * (scale * pair_inv)

    def two(slot, columns):
        for i, column in enumerate(columns):
            cot_v[i, :outputs, :LANES] = gradient(
                own_ref[slot + i].astype(jnp.float32),
                other_ref[slot + i].astype(jnp.float32),
                target_ref[column, :, :LANES].astype(jnp.float32),
                half_weight[:, :LANES],
                slice(0, LANES),
            )
            tails_v[i, :, :tail] = target_ref[column, :, LANES:].astype(jnp.float32)
        block = total + slot // 2
        ends = gradient(
            own_ref[block].astype(jnp.float32),
            other_ref[block].astype(jnp.float32),
            together(tails_v[0], tails_v[1]),
            half_weight[:, LANES:] if len(columns) == 2 else single_weight,
            slice(LANES, 2 * LANES),
        )
        cot_v[0, :outputs, LANES:rows] = ends[:, :tail]
        if len(columns) == 2:
            cot_v[1, :outputs, LANES:rows] = pltpu.roll(ends, LANES // 2, 1)[:, :tail]
        for i, column in enumerate(columns):
            cot = cot_v[i]
            turned_v[slot + i] = cot.T[:rows].astype(jnp.bfloat16)
            cot = cot[:outputs]
            shifted = jnp.concatenate(
                [pltpu.roll(cot, RING - 1, 1), cot, pltpu.roll(cot, 1, 1)], axis=0
            )
            acc_v[...] += jnp.dot(
                shifted.astype(jnp.bfloat16),
                window(field, edges, column),
                preferred_element_type=jnp.float32,
            )

    lane = lax.broadcasted_iota(jnp.int32, (1, LANES), 1)
    single_weight = jnp.where(lane < LANES // 2, half_weight[:, LANES:], 0.0)
    each_pair(start, count, wraps, two, turned_v, turned_out, sems)
    for a in range(3):
        for b in range(3):
            block = acc_v[a * outputs : (a + 1) * outputs, b * inputs : (b + 1) * inputs]
            place = slice((3 * a + b) * outputs, (3 * a + b + 1) * outputs)
            sums_out[place] = block + sums_ref[place] if adds else block
    spare = slice(9 * outputs, sums_out.shape[0])
    whole = jnp.sum(score_v[...], axis=1, keepdims=True)
    filler = jnp.broadcast_to(whole, (sums_out.shape[0] - 9 * outputs, inputs))
    sums_out[spare] = filler + sums_ref[spare] if adds else filler


def scored(start, count, wraps, field, own, other, target, weight, edges, carried, sum_rows):
    columns, outputs, rows = target.shape
    inputs = field[0].shape[2]
    total = count + wraps
    edges = list(edges) if wraps else []
    given = [*field, own, other, target, weight, *edges]
    in_specs = [VMEM] * len(given)
    aliases = {}
    if carried is not None:
        turned, sums = carried
        aliases = {len(given) + 1: 0}
        given += [sums, turned]
        in_specs += [VMEM, ANY]
    return pl.pallas_call(
        functools.partial(
            score_kernel, start, count, wraps, len(edges), carried is not None, len(given)
        ),
        out_shape=(
            jax.ShapeDtypeStruct((columns, rows, LANES), jnp.bfloat16),
            jax.ShapeDtypeStruct((sum_rows, inputs), jnp.float32),
        ),
        in_specs=in_specs,
        out_specs=(ANY, VMEM),
        scratch_shapes=[
            pltpu.VMEM((2, LANES, RING), jnp.float32),
            pltpu.VMEM((3 * outputs, 3 * inputs), jnp.float32),
            pltpu.VMEM((1, 2 * LANES), jnp.float32),
            pltpu.VMEM((2, outputs, LANES), jnp.float32),
            pltpu.VMEM((total, rows, LANES), jnp.bfloat16),
            pltpu.SemaphoreType.DMA((4,)),
        ],
        input_output_aliases=aliases,
        compiler_params=pltpu.CompilerParams(vmem_limit_bytes=24 << 20),
        cost_estimate=pl.CostEstimate(
            flops=2 * total * 9 * inputs * outputs * RING,
            bytes_accessed=total * RING * (inputs + 3 * outputs) * 2,
            transcendentals=2 * total * rows,
        ),
        name="score",
    )(*given)


def backward_kernel(block, *refs):
    field, west_ref, east_ref, taps_ref, slope_out, weights_v = refs[:3], *refs[3:]
    rows, inputs = slope_out.shape[1:]
    columns = field[0].shape[0]
    outputs = taps_ref.shape[2]
    base = pl.program_id(0) * block

    @pl.when(pl.program_id(0) == 0)
    def _():
        spare = jnp.zeros((LANES - outputs, inputs), weights_v.dtype)
        for b in range(3):
            row = [jnp.concatenate([taps_ref[2 - a, 2 - b], spare], axis=0) for a in range(3)]
            weights_v[b * LANES : (b + 1) * LANES] = jnp.concatenate(row, axis=1)

    def halo_column(j):
        at = base + j
        inner = ring_column(field, (), jnp.clip(at, 0, columns - 1))
        if j == -1:
            return jnp.where(at < 0, west_ref[0], inner)
        return jnp.where(at == columns, east_ref[0], inner) if j == block else inner

    ring = [halo_column(j) for j in range(-1, block + 1)]
    for j in range(block):
        z = jnp.dot(
            jnp.concatenate(ring[j : j + 3], axis=1),
            weights_v[...],
            preferred_element_type=jnp.float32,
        )
        slope = (
            pltpu.roll(z[:, :inputs], 1, 0)
            + z[:, inputs : 2 * inputs]
            + pltpu.roll(z[:, 2 * inputs :], RING - 1, 0)
        )
        slope_out[j] = slope[:rows].astype(jnp.bfloat16)


def backward(field, edges, taps):
    columns, rows = field[0].shape[:2]
    inputs = taps.shape[3]
    block = max(n for n in range(1, 6) if columns % n == 0)
    return pl.pallas_call(
        functools.partial(backward_kernel, block),
        grid=(columns // block,),
        out_shape=jax.ShapeDtypeStruct((columns, rows, inputs), jnp.bfloat16),
        in_specs=[VMEM] * 6,
        out_specs=pl.BlockSpec((block, rows, inputs), lambda i: (i, 0, 0)),
        scratch_shapes=[
            pltpu.VMEM((3 * LANES, 3 * inputs), jnp.bfloat16),
        ],
        compiler_params=pltpu.CompilerParams(vmem_limit_bytes=24 << 20),
        cost_estimate=pl.CostEstimate(
            flops=2 * columns * 9 * inputs * LANES * RING,
            bytes_accessed=columns * RING * (inputs + LANES) * 2,
            transcendentals=0,
        ),
        name="backward",
    )(*field, *edges, taps)


def exchange(blocks):
    return lax.all_to_all(blocks, AXES, 0, 0, tiled=True)


def split(columns):
    shares = (12, 20, 13)
    edges = [1]
    for i in range(len(shares) - 1):
        edges.append(1 + 2 * round(columns * sum(shares[: i + 1]) / sum(shares) / 2))
    edges.append(columns)
    return [(low, high - low) for low, high in zip(edges, edges[1:])]


def local(features, present_condition, target, filter_weights_tensor):
    lat_rows, lon_cols, inputs = features.shape[1:]
    outputs = target.shape[2]
    total_rows = lat_rows * lax.axis_size("lat")
    total_cols = lon_cols * lax.axis_size("lon")
    devices = math.prod(lax.axis_size(axis) for axis in AXES)

    taps = jnp.transpose(filter_weights_tensor, (0, 1, 3, 2))
    row_index = lax.axis_index("lat") * lat_rows + jnp.arange(lat_rows, dtype=jnp.int32)
    weight = latitude_weights(row_index, total_rows)
    ends = jnp.pad(weight[LANES:], (0, LANES + LANES // 2 - lat_rows))
    weight = jnp.concatenate([weight[:LANES], ends, ends])[None]
    columns = jnp.transpose(features[0], (1, 0, 2))
    present = jnp.transpose(present_condition[0], (1, 2, 0))
    truth = jnp.transpose(target, (1, 2, 0))

    field = (columns, *lat_edges(columns))
    rings = lon_rings(*field)
    edges = None
    chunks = split(lon_cols)
    pred = None
    packed = []
    for start, count in chunks:
        wraps = int(start + count == lon_cols)
        if wraps:
            edges = lon_edges(rings)
        pred, own = forward(start, count, wraps, field, present, taps, edges, pred)
        if not wraps:
            rings, own = lax.optimization_barrier((rings, own))
        packed.append((own, lax.ppermute(own, "member", [(0, 1), (1, 0)])))

    width = -(-(9 * outputs * inputs + 1) // (devices * LANES)) * LANES
    sum_rows = devices * width // inputs
    carried = None
    for (start, count), (own, other) in zip(chunks, packed):
        wraps = int(start + count == lon_cols)
        carried = scored(
            start, count, wraps, field, own, other, truth, weight, edges, carried, sum_rows
        )
    turned, sums = carried
    share = jnp.sum(exchange(sums.reshape(devices, width)), axis=0, keepdims=True)
    field = (turned, *lat_edges(turned))
    share, edges = lax.optimization_barrier((share, lon_edges(lon_rings(*field))))
    whole = exchange(jnp.broadcast_to(share, (devices, width))).reshape(sum_rows, inputs)
    slope = backward(field, edges, taps)
    objective_mean = whole[9 * outputs, 0] / (total_rows * total_cols)
    summed = whole[: 9 * outputs] / math.sqrt(2.0 * total_rows * total_cols)
    filter_weights_slope = jnp.transpose(summed.reshape(3, 3, outputs, inputs), (0, 1, 3, 2))
    return (
        jnp.transpose(pred, (2, 0, 1))[None],
        objective_mean,
        jnp.transpose(slope, (1, 0, 2))[None],
        filter_weights_slope,
    )


def solution(mesh):
    in_specs = (
        P("member", "lat", "lon", None),
        P("member", "lat", "lon", None),
        P("lat", "lon", None),
        P(),
    )
    out_specs = (P("member", "lat", "lon", None), P(), P("member", "lat", "lon", None), P())
    return jax.shard_map(local, mesh=mesh, in_specs=in_specs, out_specs=out_specs, check_vma=False)
```

```python
import functools
import math

import jax
import jax.numpy as jnp
from jax import lax
from jax.experimental import pallas as pl
from jax.experimental.pallas import tpu as pltpu
from jax.sharding import PartitionSpec as P

epsilon = 1e-06
RING = 256
LANES = 128
TILE = 16
AXES = ("member", "lat", "lon")
VMEM = pl.BlockSpec(memory_space=pltpu.VMEM)
ANY = pl.BlockSpec(memory_space=pl.ANY)


def latitude_weights(row_index, total_rows):
    scale = math.pi / total_rows
    angles = 0.5 * math.pi - (row_index.astype(jnp.float32) + 0.5) * scale
    mean = sum(math.cos(0.5 * math.pi - (r + 0.5) * scale) for r in range(total_rows)) / total_rows
    return jnp.cos(angles) * (1.0 / mean)


def swapped(first, last, axis, wraps):
    count = lax.axis_size(axis)
    even = lax.axis_index(axis) % 2 == 0
    inner = [(i, i + 1) for i in range(0, count, 2)]
    outer = [(i, (i + 1) % count) for i in range(1, count, 2) if wraps or i + 1 < count]
    both = [pairs + [(j, i) for i, j in pairs] for pairs in (inner, outer)]
    near = lax.ppermute(jnp.where(even, last, first), axis, both[0])
    far = lax.ppermute(jnp.where(even, first, last), axis, both[1])
    return jnp.where(even, far, near), jnp.where(even, near, far)


def lat_edges(columns):
    count, rows, channels = columns.shape
    body = rows - rows % TILE
    above, below = swapped(columns[:, :1], columns[:, rows - 1 :], "lat", False)
    gap = jnp.zeros((count, TILE - 1, channels), columns.dtype)
    low = jnp.concatenate([columns[:, body:], below, gap[:, : TILE - 1 - (rows - body)]], axis=1)
    return low, jnp.concatenate([gap, above], axis=1)


def lon_rings(columns, low, high):
    body = columns.shape[1] - columns.shape[1] % TILE

    def ring(part):
        gap = jnp.zeros((1, RING - body - 2 * TILE, columns.shape[2]), columns.dtype)
        return jnp.concatenate([columns[part, :body], low[part], gap, high[part]], axis=1)

    return ring(slice(0, 1)), ring(slice(-1, None))


def lon_edges(rings):
    return swapped(*rings, "lon", True)


def ring_column(field, edges, column):
    field_ref, low_ref, high_ref = field
    if isinstance(column, int) and not 0 <= column < field_ref.shape[0]:
        return edges[0 if column < 0 else 1][0]
    body = field_ref.shape[1] - field_ref.shape[1] % TILE
    gap = jnp.zeros((RING - body - 2 * TILE, field_ref.shape[2]), field_ref.dtype)
    return jnp.concatenate([field_ref[column, :body], low_ref[column], gap, high_ref[column]], axis=0)


def window(field, edges, column):
    return jnp.concatenate([ring_column(field, edges, column + b - 1) for b in range(3)], axis=1)


def each_pair(start, count, wraps, two, source_v, out, sems):
    total = count + wraps
    pairs = (count - wraps) // 2

    def pair(t, carry):
        two(2 * t, (start + 2 * t, start + 2 * t + 1))
        to = out.at[pl.ds(start + 2 * t, 2)]
        pltpu.make_async_copy(source_v.at[pl.ds(2 * t, 2)], to, sems.at[0]).start()
        return carry

    lax.fori_loop(0, pairs, pair, 0)
    copies = []
    if pairs:
        span = pl.ds(0, 2 * pairs), pl.ds(start, 2 * pairs)
        copies.append(pltpu.make_async_copy(source_v.at[span[0]], out.at[span[1]], sems.at[0]))
    columns = [start + slot if slot < count else 0 for slot in range(total)]
    for slot in range(2 * pairs, total, 2):
        two(slot, tuple(columns[slot : slot + 2]))
        for i in range(slot, min(slot + 2, total)):
            copy = pltpu.make_async_copy(
                source_v.at[pl.ds(i, 1)], out.at[pl.ds(columns[i], 1)], sems.at[1 + i - 2 * pairs]
            )
            copy.start()
            copies.append(copy)
    for copy in copies:
        copy.wait()


def together(low, high):
    lane = lax.broadcasted_iota(jnp.int32, low.shape, 1)
    return jnp.where(lane < LANES // 2, low, pltpu.roll(high, LANES // 2, 1))


def forward_kernel(start, count, wraps, n_given, *refs):
    field, present_ref, taps_ref = refs[:3], refs[3], refs[4]
    edges = refs[5:7] if wraps else ()
    pred_out, packed_out, weights_v, tails_v, pred_v, sems = refs[n_given:]
    outputs, rows = present_ref.shape[1:]
    for a in range(3):
        weights_v[a * outputs : (a + 1) * outputs] = jnp.concatenate(
            [taps_ref[a, b] for b in range(3)], axis=1
        )
    total = count + wraps
    tails_v[...] = jnp.zeros_like(tails_v)

    def one(slot, column, odd):
        y = lax.dot_general(
            weights_v[...],
            window(field, edges, column),
            (((1,), (1,)), ((), ())),
            preferred_element_type=jnp.float32,
        )
        increment = (
            pltpu.roll(y[:outputs], 1, 1)
            + y[outputs : 2 * outputs]
            + pltpu.roll(y[2 * outputs :], RING - 1, 1)
        )
        head = increment[:, :LANES] + present_ref[column, :, :LANES].astype(jnp.float32)
        tail = increment[:, LANES:rows] + present_ref[column, :, LANES:].astype(jnp.float32)
        head = head.astype(jnp.bfloat16)
        tail = tail.astype(jnp.bfloat16)
        pred_v[slot, :, :LANES] = head
        pred_v[slot, :, LANES:] = tail
        packed_out[slot] = head
        tails_v[odd, :, : rows - LANES] = tail.astype(jnp.float32)

    def two(slot, columns):
        for i, column in enumerate(columns):
            one(slot + i, column, i)
        packed_out[total + slot // 2] = together(tails_v[0], tails_v[1]).astype(jnp.bfloat16)

    each_pair(start, count, wraps, two, pred_v, pred_out, sems)


def forward(start, count, wraps, field, present, taps, edges, pred):
    columns, outputs, rows = present.shape
    inputs = taps.shape[3]
    total = count + wraps
    given = [*field, present, taps] + (list(edges) if wraps else [])
    in_specs = [VMEM] * len(given)
    aliases = {}
    if pred is not None:
        aliases = {len(given): 0}
        given.append(pred)
        in_specs.append(ANY)
    return pl.pallas_call(
        functools.partial(forward_kernel, start, count, wraps, len(given)),
        out_shape=(
            jax.ShapeDtypeStruct((columns, outputs, rows), jnp.bfloat16),
            jax.ShapeDtypeStruct((total + (total + 1) // 2, outputs, LANES), jnp.bfloat16),
        ),
        in_specs=in_specs,
        out_specs=(ANY, VMEM),
        scratch_shapes=[
            pltpu.VMEM((3 * outputs, 3 * inputs), jnp.bfloat16),
            pltpu.VMEM((2, outputs, LANES), jnp.float32),
            pltpu.VMEM((total, outputs, rows), jnp.bfloat16),
            pltpu.SemaphoreType.DMA((4,)),
        ],
        input_output_aliases=aliases,
        compiler_params=pltpu.CompilerParams(vmem_limit_bytes=24 << 20),
        cost_estimate=pl.CostEstimate(
            flops=2 * total * 9 * inputs * outputs * RING,
            bytes_accessed=total * RING * (inputs + 3 * outputs) * 2,
            transcendentals=0,
        ),
        name="forward",
    )(*given)


def score_kernel(start, count, wraps, n_edges, adds, n_given, *refs):
    field, own_ref, other_ref, target_ref, weight_ref = refs[:3], *refs[3:7]
    edges = refs[7 : 7 + n_edges]
    sums_ref = refs[7 + n_edges] if adds else None
    turned_out, sums_out, cot_v, acc_v, score_v, tails_v, turned_v, sems = refs[n_given:]
    outputs, rows = target_ref.shape[1:]
    inputs = field[0].shape[2]
    total = count + wraps
    tail = rows - LANES
    half_weight = 0.5 * weight_ref[...]
    cot_v[...] = jnp.zeros_like(cot_v)
    acc_v[...] = jnp.zeros_like(acc_v)
    score_v[...] = jnp.zeros_like(score_v)
    tails_v[...] = jnp.zeros_like(tails_v)

    def gradient(value, partner, truth, scale, lanes):
        misfit = value - truth
        spread = value - partner
        error2 = jnp.sum(misfit * misfit, axis=0, keepdims=True) + epsilon
        pair2 = jnp.sum(spread * spread, axis=0, keepdims=True) + epsilon
        error_inv = lax.rsqrt(error2)
        pair_inv = lax.rsqrt(pair2)
        score_v[:, lanes] += scale * (error2 * error_inv - 0.5 * (pair2 * pair_inv))
        return misfit * (scale * error_inv) - spread * (scale * pair_inv)

    def two(slot, columns):
        for i, column in enumerate(columns):
            cot_v[i, :outputs, :LANES] = gradient(
                own_ref[slot + i].astype(jnp.float32),
                other_ref[slot + i].astype(jnp.float32),
                target_ref[column, :, :LANES].astype(jnp.float32),
                half_weight[:, :LANES],
                slice(0, LANES),
            )
            tails_v[i, :, :tail] = target_ref[column, :, LANES:].astype(jnp.float32)
        block = total + slot // 2
        ends = gradient(
            own_ref[block].astype(jnp.float32),
            other_ref[block].astype(jnp.float32),
            together(tails_v[0], tails_v[1]),
            half_weight[:, LANES:] if len(columns) == 2 else single_weight,
            slice(LANES, 2 * LANES),
        )
        cot_v[0, :outputs, LANES:rows] = ends[:, :tail]
        if len(columns) == 2:
            cot_v[1, :outputs, LANES:rows] = pltpu.roll(ends, LANES // 2, 1)[:, :tail]
        for i, column in enumerate(columns):
            cot = cot_v[i]
            turned_v[slot + i] = cot.T[:rows].astype(jnp.bfloat16)
            cot = cot[:outputs]
            shifted = jnp.concatenate(
                [pltpu.roll(cot, RING - 1, 1), cot, pltpu.roll(cot, 1, 1)], axis=0
            )
            acc_v[...] += jnp.dot(
                shifted.astype(jnp.bfloat16),
                window(field, edges, column),
                preferred_element_type=jnp.float32,
            )

    lane = lax.broadcasted_iota(jnp.int32, (1, LANES), 1)
    single_weight = jnp.where(lane < LANES // 2, half_weight[:, LANES:], 0.0)
    each_pair(start, count, wraps, two, turned_v, turned_out, sems)
    for a in range(3):
        for b in range(3):
            block = acc_v[a * outputs : (a + 1) * outputs, b * inputs : (b + 1) * inputs]
            place = slice((3 * a + b) * outputs, (3 * a + b + 1) * outputs)
            sums_out[place] = block + sums_ref[place] if adds else block
    spare = slice(9 * outputs, sums_out.shape[0])
    whole = jnp.sum(score_v[...], axis=1, keepdims=True)
    filler = jnp.broadcast_to(whole, (sums_out.shape[0] - 9 * outputs, inputs))
    sums_out[spare] = filler + sums_ref[spare] if adds else filler


def scored(start, count, wraps, field, own, other, target, weight, edges, carried, sum_rows):
    columns, outputs, rows = target.shape
    inputs = field[0].shape[2]
    total = count + wraps
    edges = list(edges) if wraps else []
    given = [*field, own, other, target, weight, *edges]
    in_specs = [VMEM] * len(given)
    aliases = {}
    if carried is not None:
        turned, sums = carried
        aliases = {len(given) + 1: 0}
        given += [sums, turned]
        in_specs += [VMEM, ANY]
    return pl.pallas_call(
        functools.partial(
            score_kernel, start, count, wraps, len(edges), carried is not None, len(given)
        ),
        out_shape=(
            jax.ShapeDtypeStruct((columns, rows, LANES), jnp.bfloat16),
            jax.ShapeDtypeStruct((sum_rows, inputs), jnp.float32),
        ),
        in_specs=in_specs,
        out_specs=(ANY, VMEM),
        scratch_shapes=[
            pltpu.VMEM((2, LANES, RING), jnp.float32),
            pltpu.VMEM((3 * outputs, 3 * inputs), jnp.float32),
            pltpu.VMEM((1, 2 * LANES), jnp.float32),
            pltpu.VMEM((2, outputs, LANES), jnp.float32),
            pltpu.VMEM((total, rows, LANES), jnp.bfloat16),
            pltpu.SemaphoreType.DMA((4,)),
        ],
        input_output_aliases=aliases,
        compiler_params=pltpu.CompilerParams(vmem_limit_bytes=24 << 20),
        cost_estimate=pl.CostEstimate(
            flops=2 * total * 9 * inputs * outputs * RING,
            bytes_accessed=total * RING * (inputs + 3 * outputs) * 2,
            transcendentals=2 * total * rows,
        ),
        name="score",
    )(*given)


def backward_kernel(block, *refs):
    field, west_ref, east_ref, taps_ref, slope_out, weights_v = refs[:3], *refs[3:]
    rows, inputs = slope_out.shape[1:]
    columns = field[0].shape[0]
    outputs = taps_ref.shape[2]
    base = pl.program_id(0) * block

    @pl.when(pl.program_id(0) == 0)
    def _():
        spare = jnp.zeros((LANES - outputs, inputs), weights_v.dtype)
        for b in range(3):
            row = [jnp.concatenate([taps_ref[2 - a, 2 - b], spare], axis=0) for a in range(3)]
            weights_v[b * LANES : (b + 1) * LANES] = jnp.concatenate(row, axis=1)

    def halo_column(j):
        at = base + j
        inner = ring_column(field, (), jnp.clip(at, 0, columns - 1))
        if j == -1:
            return jnp.where(at < 0, west_ref[0], inner)
        return jnp.where(at == columns, east_ref[0], inner) if j == block else inner

    ring = [halo_column(j) for j in range(-1, block + 1)]
    for j in range(block):
        z = jnp.dot(
            jnp.concatenate(ring[j : j + 3], axis=1),
            weights_v[...],
            preferred_element_type=jnp.float32,
        )
        slope = (
            pltpu.roll(z[:, :inputs], 1, 0)
            + z[:, inputs : 2 * inputs]
            + pltpu.roll(z[:, 2 * inputs :], RING - 1, 0)
        )
        slope_out[j] = slope[:rows].astype(jnp.bfloat16)


def backward(field, edges, taps):
    columns, rows = field[0].shape[:2]
    inputs = taps.shape[3]
    block = max(n for n in range(1, 6) if columns % n == 0)
    return pl.pallas_call(
        functools.partial(backward_kernel, block),
        grid=(columns // block,),
        out_shape=jax.ShapeDtypeStruct((columns, rows, inputs), jnp.bfloat16),
        in_specs=[VMEM] * 6,
        out_specs=pl.BlockSpec((block, rows, inputs), lambda i: (i, 0, 0)),
        scratch_shapes=[
            pltpu.VMEM((3 * LANES, 3 * inputs), jnp.bfloat16),
        ],
        compiler_params=pltpu.CompilerParams(vmem_limit_bytes=24 << 20),
        cost_estimate=pl.CostEstimate(
            flops=2 * columns * 9 * inputs * LANES * RING,
            bytes_accessed=columns * RING * (inputs + LANES) * 2,
            transcendentals=0,
        ),
        name="backward",
    )(*field, *edges, taps)


def exchange(blocks):
    return lax.all_to_all(blocks, AXES, 0, 0, tiled=True)


def split(columns):
    shares = (12, 20, 13)
    edges = [1]
    for i in range(len(shares) - 1):
        edges.append(1 + 2 * round(columns * sum(shares[: i + 1]) / sum(shares) / 2))
    edges.append(columns)
    return [(low, high - low) for low, high in zip(edges, edges[1:])]


def local(features, present_condition, target, filter_weights_tensor):
    lat_rows, lon_cols, inputs = features.shape[1:]
    outputs = target.shape[2]
    total_rows = lat_rows * lax.axis_size("lat")
    total_cols = lon_cols * lax.axis_size("lon")
    devices = math.prod(lax.axis_size(axis) for axis in AXES)

    taps = jnp.transpose(filter_weights_tensor, (0, 1, 3, 2))
    row_index = lax.axis_index("lat") * lat_rows + jnp.arange(lat_rows, dtype=jnp.int32)
    weight = latitude_weights(row_index, total_rows)
    ends = jnp.pad(weight[LANES:], (0, LANES + LANES // 2 - lat_rows))
    weight = jnp.concatenate([weight[:LANES], ends, ends])[None]
    columns = jnp.transpose(features[0], (1, 0, 2))
    present = jnp.transpose(present_condition[0], (1, 2, 0))
    truth = jnp.transpose(target, (1, 2, 0))

    field = (columns, *lat_edges(columns))
    rings = lon_rings(*field)
    edges = None
    chunks = split(lon_cols)
    width = -(-(9 * outputs * inputs + 1) // (devices * LANES)) * LANES
    sum_rows = devices * width // inputs
    pred = carried = None
    packed = []

    def score_next(carried, edges):
        (start, count), (own, other) = packed.pop(0)
        wraps = int(start + count == lon_cols)
        return scored(
            start, count, wraps, field, own, other, truth, weight, edges, carried, sum_rows
        )

    for start, count in chunks:
        wraps = int(start + count == lon_cols)
        if wraps:
            edges = lon_edges(rings)
            carried = score_next(carried, edges)
            pred, carried = lax.optimization_barrier((pred, carried))
        pred, own = forward(start, count, wraps, field, present, taps, edges, pred)
        packed.append(((start, count), (own, lax.ppermute(own, "member", [(0, 1), (1, 0)]))))
    while packed:
        carried = score_next(carried, edges)
    turned, sums = carried
    share = jnp.sum(exchange(sums.reshape(devices, width)), axis=0, keepdims=True)
    field = (turned, *lat_edges(turned))
    share, edges = lax.optimization_barrier((share, lon_edges(lon_rings(*field))))
    whole = exchange(jnp.broadcast_to(share, (devices, width))).reshape(sum_rows, inputs)
    slope = backward(field, edges, taps)
    objective_mean = whole[9 * outputs, 0] / (total_rows * total_cols)
    summed = whole[: 9 * outputs] / math.sqrt(2.0 * total_rows * total_cols)
    filter_weights_slope = jnp.transpose(summed.reshape(3, 3, outputs, inputs), (0, 1, 3, 2))
    return (
        jnp.transpose(pred, (2, 0, 1))[None],
        objective_mean,
        jnp.transpose(slope, (1, 0, 2))[None],
        filter_weights_slope,
    )


def solution(mesh):
    in_specs = (
        P("member", "lat", "lon", None),
        P("member", "lat", "lon", None),
        P("lat", "lon", None),
        P(),
    )
    out_specs = (P("member", "lat", "lon", None), P(), P("member", "lat", "lon", None), P())
    return jax.shard_map(local, mesh=mesh, in_specs=in_specs, out_specs=out_specs, check_vma=False)
```

```python
import functools
import math

import jax
import jax.numpy as jnp
from jax import lax
from jax.experimental import pallas as pl
from jax.experimental.pallas import tpu as pltpu
from jax.sharding import PartitionSpec as P

epsilon = 1e-06
RING = 256
LANES = 128
TILE = 16
AXES = ("member", "lat", "lon")
VMEM = pl.BlockSpec(memory_space=pltpu.VMEM)
ANY = pl.BlockSpec(memory_space=pl.ANY)


def latitude_weights(row_index, total_rows):
    scale = math.pi / total_rows
    angles = 0.5 * math.pi - (row_index.astype(jnp.float32) + 0.5) * scale
    mean = sum(math.cos(0.5 * math.pi - (r + 0.5) * scale) for r in range(total_rows)) / total_rows
    return jnp.cos(angles) * (1.0 / mean)


def swapped(first, last, axis, wraps):
    count = lax.axis_size(axis)
    even = lax.axis_index(axis) % 2 == 0
    inner = [(i, i + 1) for i in range(0, count, 2)]
    outer = [(i, (i + 1) % count) for i in range(1, count, 2) if wraps or i + 1 < count]
    both = [pairs + [(j, i) for i, j in pairs] for pairs in (inner, outer)]
    near = lax.ppermute(jnp.where(even, last, first), axis, both[0])
    far = lax.ppermute(jnp.where(even, first, last), axis, both[1])
    return jnp.where(even, far, near), jnp.where(even, near, far)


def lat_edges(columns):
    count, rows, channels = columns.shape
    body = rows - rows % TILE
    above, below = swapped(columns[:, :1], columns[:, rows - 1 :], "lat", False)
    gap = jnp.zeros((count, TILE - 1, channels), columns.dtype)
    low = jnp.concatenate([columns[:, body:], below, gap[:, : TILE - 1 - (rows - body)]], axis=1)
    return low, jnp.concatenate([gap, above], axis=1)


def lon_rings(columns, low, high):
    body = columns.shape[1] - columns.shape[1] % TILE

    def ring(part):
        gap = jnp.zeros((1, RING - body - 2 * TILE, columns.shape[2]), columns.dtype)
        return jnp.concatenate([columns[part, :body], low[part], gap, high[part]], axis=1)

    return ring(slice(0, 1)), ring(slice(-1, None))


def lon_edges(rings):
    return swapped(*rings, "lon", True)


def ring_column(field, edges, column):
    field_ref, low_ref, high_ref = field
    if isinstance(column, int) and not 0 <= column < field_ref.shape[0]:
        return edges[0 if column < 0 else 1][0]
    body = field_ref.shape[1] - field_ref.shape[1] % TILE
    gap = jnp.zeros((RING - body - 2 * TILE, field_ref.shape[2]), field_ref.dtype)
    return jnp.concatenate([field_ref[column, :body], low_ref[column], gap, high_ref[column]], axis=0)


def window(field, edges, column):
    return jnp.concatenate([ring_column(field, edges, column + b - 1) for b in range(3)], axis=1)


def each_pair(start, count, wraps, two, source_v, out, sems):
    total = count + wraps
    pairs = (count - wraps) // 2

    def pair(t, carry):
        two(2 * t, (start + 2 * t, start + 2 * t + 1))
        to = out.at[pl.ds(start + 2 * t, 2)]
        pltpu.make_async_copy(source_v.at[pl.ds(2 * t, 2)], to, sems.at[0]).start()
        return carry

    lax.fori_loop(0, pairs, pair, 0)
    copies = []
    if pairs:
        span = pl.ds(0, 2 * pairs), pl.ds(start, 2 * pairs)
        copies.append(pltpu.make_async_copy(source_v.at[span[0]], out.at[span[1]], sems.at[0]))
    columns = [start + slot if slot < count else 0 for slot in range(total)]
    for slot in range(2 * pairs, total, 2):
        two(slot, tuple(columns[slot : slot + 2]))
        for i in range(slot, min(slot + 2, total)):
            copy = pltpu.make_async_copy(
                source_v.at[pl.ds(i, 1)], out.at[pl.ds(columns[i], 1)], sems.at[1 + i - 2 * pairs]
            )
            copy.start()
            copies.append(copy)
    for copy in copies:
        copy.wait()


def together(low, high):
    lane = lax.broadcasted_iota(jnp.int32, low.shape, 1)
    return jnp.where(lane < LANES // 2, low, pltpu.roll(high, LANES // 2, 1))


def forward_kernel(start, count, wraps, n_given, *refs):
    field, present_ref, taps_ref = refs[:3], refs[3], refs[4]
    edges = refs[5:7] if wraps else ()
    pred_out, packed_out, weights_v, tails_v, pred_v, sems = refs[n_given:]
    outputs, rows = present_ref.shape[1:]
    for a in range(3):
        weights_v[a * outputs : (a + 1) * outputs] = jnp.concatenate(
            [taps_ref[a, b] for b in range(3)], axis=1
        )
    total = count + wraps
    tails_v[...] = jnp.zeros_like(tails_v)

    def one(slot, column, odd):
        y = lax.dot_general(
            weights_v[...],
            window(field, edges, column),
            (((1,), (1,)), ((), ())),
            preferred_element_type=jnp.float32,
        )
        increment = (
            pltpu.roll(y[:outputs], 1, 1)
            + y[outputs : 2 * outputs]
            + pltpu.roll(y[2 * outputs :], RING - 1, 1)
        )
        head = increment[:, :LANES] + present_ref[column, :, :LANES].astype(jnp.float32)
        tail = increment[:, LANES:rows] + present_ref[column, :, LANES:].astype(jnp.float32)
        head = head.astype(jnp.bfloat16)
        tail = tail.astype(jnp.bfloat16)
        pred_v[slot, :, :LANES] = head
        pred_v[slot, :, LANES:] = tail
        packed_out[slot] = head
        tails_v[odd, :, : rows - LANES] = tail.astype(jnp.float32)

    def two(slot, columns):
        for i, column in enumerate(columns):
            one(slot + i, column, i)
        packed_out[total + slot // 2] = together(tails_v[0], tails_v[1]).astype(jnp.bfloat16)

    each_pair(start, count, wraps, two, pred_v, pred_out, sems)


def forward(start, count, wraps, field, present, taps, edges, pred):
    columns, outputs, rows = present.shape
    inputs = taps.shape[3]
    total = count + wraps
    given = [*field, present, taps] + (list(edges) if wraps else [])
    in_specs = [VMEM] * len(given)
    aliases = {}
    if pred is not None:
        aliases = {len(given): 0}
        given.append(pred)
        in_specs.append(ANY)
    return pl.pallas_call(
        functools.partial(forward_kernel, start, count, wraps, len(given)),
        out_shape=(
            jax.ShapeDtypeStruct((columns, outputs, rows), jnp.bfloat16),
            jax.ShapeDtypeStruct((total + (total + 1) // 2, outputs, LANES), jnp.bfloat16),
        ),
        in_specs=in_specs,
        out_specs=(ANY, VMEM),
        scratch_shapes=[
            pltpu.VMEM((3 * outputs, 3 * inputs), jnp.bfloat16),
            pltpu.VMEM((2, outputs, LANES), jnp.float32),
            pltpu.VMEM((total, outputs, rows), jnp.bfloat16),
            pltpu.SemaphoreType.DMA((4,)),
        ],
        input_output_aliases=aliases,
        compiler_params=pltpu.CompilerParams(vmem_limit_bytes=24 << 20),
        cost_estimate=pl.CostEstimate(
            flops=2 * total * 9 * inputs * outputs * RING,
            bytes_accessed=total * RING * (inputs + 3 * outputs) * 2,
            transcendentals=0,
        ),
        name="forward",
    )(*given)


def score_kernel(start, count, wraps, n_edges, adds, n_given, *refs):
    field, own_ref, other_ref, target_ref, weight_ref = refs[:3], *refs[3:7]
    edges = refs[7 : 7 + n_edges]
    sums_ref = refs[7 + n_edges] if adds else None
    turned_out, sums_out, cot_v, acc_v, score_v, tails_v, turned_v, sems = refs[n_given:]
    outputs, rows = target_ref.shape[1:]
    inputs = field[0].shape[2]
    total = count + wraps
    tail = rows - LANES
    half_weight = 0.5 * weight_ref[...]
    cot_v[...] = jnp.zeros_like(cot_v)
    acc_v[...] = jnp.zeros_like(acc_v)
    score_v[...] = jnp.zeros_like(score_v)
    tails_v[...] = jnp.zeros_like(tails_v)

    def gradient(value, partner, truth, scale, lanes):
        misfit = value - truth
        spread = value - partner
        error2 = jnp.sum(misfit * misfit, axis=0, keepdims=True) + epsilon
        pair2 = jnp.sum(spread * spread, axis=0, keepdims=True) + epsilon
        error_inv = lax.rsqrt(error2)
        pair_inv = lax.rsqrt(pair2)
        score_v[:, lanes] += scale * (error2 * error_inv - 0.5 * (pair2 * pair_inv))
        return misfit * (scale * error_inv) - spread * (scale * pair_inv)

    def two(slot, columns):
        for i, column in enumerate(columns):
            cot_v[i, :outputs, :LANES] = gradient(
                own_ref[slot + i].astype(jnp.float32),
                other_ref[slot + i].astype(jnp.float32),
                target_ref[column, :, :LANES].astype(jnp.float32),
                half_weight[:, :LANES],
                slice(0, LANES),
            )
            tails_v[i, :, :tail] = target_ref[column, :, LANES:].astype(jnp.float32)
        block = total + slot // 2
        ends = gradient(
            own_ref[block].astype(jnp.float32),
            other_ref[block].astype(jnp.float32),
            together(tails_v[0], tails_v[1]),
            half_weight[:, LANES:] if len(columns) == 2 else single_weight,
            slice(LANES, 2 * LANES),
        )
        cot_v[0, :outputs, LANES:rows] = ends[:, :tail]
        if len(columns) == 2:
            cot_v[1, :outputs, LANES:rows] = pltpu.roll(ends, LANES // 2, 1)[:, :tail]
        for i, column in enumerate(columns):
            cot = cot_v[i]
            turned_v[slot + i] = cot.T[:rows].astype(jnp.bfloat16)
            cot = cot[:outputs]
            shifted = jnp.concatenate(
                [pltpu.roll(cot, RING - 1, 1), cot, pltpu.roll(cot, 1, 1)], axis=0
            )
            acc_v[...] += jnp.dot(
                shifted.astype(jnp.bfloat16),
                window(field, edges, column),
                preferred_element_type=jnp.float32,
            )

    lane = lax.broadcasted_iota(jnp.int32, (1, LANES), 1)
    single_weight = jnp.where(lane < LANES // 2, half_weight[:, LANES:], 0.0)
    each_pair(start, count, wraps, two, turned_v, turned_out, sems)
    for a in range(3):
        for b in range(3):
            block = acc_v[a * outputs : (a + 1) * outputs, b * inputs : (b + 1) * inputs]
            place = slice((3 * a + b) * outputs, (3 * a + b + 1) * outputs)
            sums_out[place] = block + sums_ref[place] if adds else block
    spare = slice(9 * outputs, sums_out.shape[0])
    whole = jnp.sum(score_v[...], axis=1, keepdims=True)
    filler = jnp.broadcast_to(whole, (sums_out.shape[0] - 9 * outputs, inputs))
    sums_out[spare] = filler + sums_ref[spare] if adds else filler


def scored(start, count, wraps, field, own, other, target, weight, edges, carried, sum_rows):
    columns, outputs, rows = target.shape
    inputs = field[0].shape[2]
    total = count + wraps
    edges = list(edges) if wraps else []
    given = [*field, own, other, target, weight, *edges]
    in_specs = [VMEM] * len(given)
    aliases = {}
    if carried is not None:
        turned, sums = carried
        aliases = {len(given) + 1: 0}
        given += [sums, turned]
        in_specs += [VMEM, ANY]
    return pl.pallas_call(
        functools.partial(
            score_kernel, start, count, wraps, len(edges), carried is not None, len(given)
        ),
        out_shape=(
            jax.ShapeDtypeStruct((columns, rows, LANES), jnp.bfloat16),
            jax.ShapeDtypeStruct((sum_rows, inputs), jnp.float32),
        ),
        in_specs=in_specs,
        out_specs=(ANY, VMEM),
        scratch_shapes=[
            pltpu.VMEM((2, LANES, RING), jnp.float32),
            pltpu.VMEM((3 * outputs, 3 * inputs), jnp.float32),
            pltpu.VMEM((1, 2 * LANES), jnp.float32),
            pltpu.VMEM((2, outputs, LANES), jnp.float32),
            pltpu.VMEM((total, rows, LANES), jnp.bfloat16),
            pltpu.SemaphoreType.DMA((4,)),
        ],
        input_output_aliases=aliases,
        compiler_params=pltpu.CompilerParams(vmem_limit_bytes=24 << 20),
        cost_estimate=pl.CostEstimate(
            flops=2 * total * 9 * inputs * outputs * RING,
            bytes_accessed=total * RING * (inputs + 3 * outputs) * 2,
            transcendentals=2 * total * rows,
        ),
        name="score",
    )(*given)


def backward_kernel(block, *refs):
    field, west_ref, east_ref, taps_ref, slope_out, weights_v = refs[:3], *refs[3:]
    rows, inputs = slope_out.shape[1:]
    columns = field[0].shape[0]
    outputs = taps_ref.shape[2]
    base = pl.program_id(0) * block

    @pl.when(pl.program_id(0) == 0)
    def _():
        spare = jnp.zeros((LANES - outputs, inputs), weights_v.dtype)
        for b in range(3):
            row = [jnp.concatenate([taps_ref[2 - a, 2 - b], spare], axis=0) for a in range(3)]
            weights_v[b * LANES : (b + 1) * LANES] = jnp.concatenate(row, axis=1)

    def halo_column(j):
        at = base + j
        inner = ring_column(field, (), jnp.clip(at, 0, columns - 1))
        if j == -1:
            return jnp.where(at < 0, west_ref[0], inner)
        return jnp.where(at == columns, east_ref[0], inner) if j == block else inner

    ring = [halo_column(j) for j in range(-1, block + 1)]
    for j in range(block):
        z = jnp.dot(
            jnp.concatenate(ring[j : j + 3], axis=1),
            weights_v[...],
            preferred_element_type=jnp.float32,
        )
        slope = (
            pltpu.roll(z[:, :inputs], 1, 0)
            + z[:, inputs : 2 * inputs]
            + pltpu.roll(z[:, 2 * inputs :], RING - 1, 0)
        )
        slope_out[j] = slope[:rows].astype(jnp.bfloat16)


def backward(field, edges, taps):
    columns, rows = field[0].shape[:2]
    inputs = taps.shape[3]
    block = max(n for n in range(1, 6) if columns % n == 0)
    return pl.pallas_call(
        functools.partial(backward_kernel, block),
        grid=(columns // block,),
        out_shape=jax.ShapeDtypeStruct((columns, rows, inputs), jnp.bfloat16),
        in_specs=[VMEM] * 6,
        out_specs=pl.BlockSpec((block, rows, inputs), lambda i: (i, 0, 0)),
        scratch_shapes=[
            pltpu.VMEM((3 * LANES, 3 * inputs), jnp.bfloat16),
        ],
        compiler_params=pltpu.CompilerParams(vmem_limit_bytes=24 << 20),
        cost_estimate=pl.CostEstimate(
            flops=2 * columns * 9 * inputs * LANES * RING,
            bytes_accessed=columns * RING * (inputs + LANES) * 2,
            transcendentals=0,
        ),
        name="backward",
    )(*field, *edges, taps)


def exchange(blocks):
    return lax.all_to_all(blocks, AXES, 0, 0, tiled=True)


def split(columns):
    shares = (18, 16, 11)
    edges = [1]
    for i in range(len(shares) - 1):
        edges.append(1 + 2 * round(columns * sum(shares[: i + 1]) / sum(shares) / 2))
    edges.append(columns)
    return [(low, high - low) for low, high in zip(edges, edges[1:])]


def local(features, present_condition, target, filter_weights_tensor):
    lat_rows, lon_cols, inputs = features.shape[1:]
    outputs = target.shape[2]
    total_rows = lat_rows * lax.axis_size("lat")
    total_cols = lon_cols * lax.axis_size("lon")
    devices = math.prod(lax.axis_size(axis) for axis in AXES)

    taps = jnp.transpose(filter_weights_tensor, (0, 1, 3, 2))
    row_index = lax.axis_index("lat") * lat_rows + jnp.arange(lat_rows, dtype=jnp.int32)
    weight = latitude_weights(row_index, total_rows)
    ends = jnp.pad(weight[LANES:], (0, LANES + LANES // 2 - lat_rows))
    weight = jnp.concatenate([weight[:LANES], ends, ends])[None]
    columns = jnp.transpose(features[0], (1, 0, 2))
    present = jnp.transpose(present_condition[0], (1, 2, 0))
    truth = jnp.transpose(target, (1, 2, 0))

    field = (columns, *lat_edges(columns))
    rings = lon_rings(*field)
    edges = None
    chunks = split(lon_cols)
    width = -(-(9 * outputs * inputs + 1) // (devices * LANES)) * LANES
    sum_rows = devices * width // inputs
    pred = carried = None
    packed = []

    def score_next(carried, edges):
        (start, count), (own, other) = packed.pop(0)
        wraps = int(start + count == lon_cols)
        return scored(
            start, count, wraps, field, own, other, truth, weight, edges, carried, sum_rows
        )

    for start, count in chunks:
        wraps = int(start + count == lon_cols)
        if wraps:
            edges = lon_edges(rings)
            carried = score_next(carried, edges)
            pred, carried = lax.optimization_barrier((pred, carried))
        pred, own = forward(start, count, wraps, field, present, taps, edges, pred)
        packed.append(((start, count), (own, lax.ppermute(own, "member", [(0, 1), (1, 0)]))))
    while packed:
        carried = score_next(carried, edges)
    turned, sums = carried
    share = jnp.sum(exchange(sums.reshape(devices, width)), axis=0, keepdims=True)
    field = (turned, *lat_edges(turned))
    share, edges = lax.optimization_barrier((share, lon_edges(lon_rings(*field))))
    whole = exchange(jnp.broadcast_to(share, (devices, width))).reshape(sum_rows, inputs)
    slope = backward(field, edges, taps)
    objective_mean = whole[9 * outputs, 0] / (total_rows * total_cols)
    summed = whole[: 9 * outputs] / math.sqrt(2.0 * total_rows * total_cols)
    filter_weights_slope = jnp.transpose(summed.reshape(3, 3, outputs, inputs), (0, 1, 3, 2))
    return (
        jnp.transpose(pred, (2, 0, 1))[None],
        objective_mean,
        jnp.transpose(slope, (1, 0, 2))[None],
        filter_weights_slope,
    )


def solution(mesh):
    in_specs = (
        P("member", "lat", "lon", None),
        P("member", "lat", "lon", None),
        P("lat", "lon", None),
        P(),
    )
    out_specs = (P("member", "lat", "lon", None), P(), P("member", "lat", "lon", None), P())
    return jax.shard_map(local, mesh=mesh, in_specs=in_specs, out_specs=out_specs, check_vma=False)
```
